512 devices in a mesh: obs: 16 (over y, x), flux: 32 (over z, core).
Axes of the slice: x: 4, y: 4, z: 16, core: 2. Of those that a mesh axis runs over, the one named last changes fastest.
Arguments:
- ensemble: bfloat16 [131072, 256], P(('obs', 'flux')), may hold values from -6 to 6
- footprint: bfloat16 [256, 32, 8, 128, 128], P('obs', 'flux'), may hold values from -0.046875 to 0.046875
- tile_index: int32 [256, 32, 8], P('obs', 'flux'), may hold values from 0 to 31, as said below
- tile_count: int32 [256, 32], P('obs', 'flux'), may hold values from 1 to 8, as said below
- observed: float32 [32768], P(('obs', 'flux')), may hold values from -8 to 8
- obs_sigma: float32 [32768], P(('obs', 'flux')), may hold values from 3 to 30
Outputs:
- posterior: bfloat16 [131072, 256], P(('obs', 'flux'))
The draws below stay inside these ranges and needn't reach their ends.
Inputs may be any that keep to these rules, and one draw needn't show every extreme that they name: `tile_index`: the 8 tiles of one block and region are different. `tile_count`: some block and region uses all 8 slots.
All inputs are finite; a program needn't handle non-finite values.
Results may differ from the reference program's by a relative error of at most 0.0095.
Values may be sent and summed in bfloat16 or wider, within the bound.
A program may use at most 64 MiB of HBM per device.

```python
import math
import jax
import jax.numpy as jnp
from jax import lax

MEMBERS = 256
TILE = 128
SLOTS = 8
CP = 256
NBLK = 256
NOBS = 32768
CELLS = 131072
TILES_REG = 32
N_OBS = 16
N_FLUX = 32


def draw_tile_index(key, part):
    scores = jax.random.randint(key, (NBLK, N_FLUX, TILES_REG), 0, 2 ** 20)
    scores = scores * TILES_REG + jnp.arange(TILES_REG, dtype=jnp.int32)
    order = jnp.argsort(scores, axis=-1, stable=True)
    return order[:, :, :SLOTS].astype(jnp.int32)


def draw_tile_count(key, part):
    first = jax.random.fold_in(key, 11)
    second = jax.random.fold_in(key, 12)
    third = jax.random.fold_in(key, 13)
    heavy = jax.random.randint(first, (NBLK, 1), 0, 4) == 0
    many = jax.random.randint(second, (NBLK, N_FLUX), 1, SLOTS + 1)
    light = 1 + many % 2
    counts = jnp.where(heavy, many, light)
    where_full = jax.random.randint(third, (), 0, NBLK * N_FLUX)
    flat = counts.reshape(-1)
    flat = jnp.where(jnp.arange(NBLK * N_FLUX) == where_full, SLOTS, flat)
    return flat.reshape(NBLK, N_FLUX).astype(jnp.int32)


def level_of(key, dims, pieces, least, high):
    loudness, own = 1.0, jax.random.fold_in(key, 6)
    for position, shards_of in pieces:
        steps = jnp.exp(jax.random.uniform(jax.random.fold_in(own, position), (shards_of,), jnp.float32, least / len(pieces), high / len(pieces)))
        loudness = loudness * jnp.repeat(steps, dims[position] // shards_of).reshape([-1 if axis == position else 1 for axis in range(len(dims))])
    return loudness


def noise(key, extent, scale, reach, pieces=(), held_as=jnp.bfloat16):
    array = jax.random.normal(key, extent, jnp.float32) * scale
    if len(pieces) > 0:
        array = level_of(key, extent, pieces, -0.22, 0.18) * array
    return jnp.clip(array, min=-reach, max=reach).astype(held_as)


def setup_inputs(seed: int = 0) -> dict:
    keys = jax.random.split(jax.random.key(seed), 7)
    ensemble = noise(keys[0], (CELLS, MEMBERS), 1.0, 6.0, ((0, 512),))
    footprint = noise(keys[1], (NBLK, N_FLUX, SLOTS, TILE, TILE), (TILE * N_FLUX * 4) ** -0.5, 0.046875, ((0, 16), (1, 32)))
    tile_index = draw_tile_index(jax.random.fold_in(keys[6], 71), 0)
    tile_count = draw_tile_count(jax.random.fold_in(keys[6], 71), 0)
    observed = noise(keys[4], (NOBS,), 2.0, 8.0, ((0, 512),), jnp.float32)
    obs_sigma = jnp.clip(jnp.exp(math.log(30.0) - 2.3025851 * jax.random.uniform(keys[5], (NOBS,), jnp.float32) ** level_of(keys[5], (NOBS,), ((0, 512),), -0.2, 0.2)), 3.0, 30.0)
    return {"ensemble": ensemble, "footprint": footprint, "tile_index": tile_index, "tile_count": tile_count, "observed": observed, "obs_sigma": obs_sigma}


def reference(ensemble, footprint, tile_index, tile_count, observed, obs_sigma):
    regions = ensemble.reshape(N_OBS, N_FLUX, CP, MEMBERS).transpose(1, 0, 2, 3)
    regions = regions.reshape(N_FLUX, TILES_REG, TILE, MEMBERS)
    slot_ids = jnp.arange(SLOTS, dtype=jnp.int32)

    def one_region(region_id, evolved):
        region_block = lax.dynamic_index_in_dim(regions, region_id, 0, keepdims=False)
        prints = lax.dynamic_index_in_dim(footprint, region_id, 1, keepdims=False)
        chosen = lax.dynamic_index_in_dim(tile_index, region_id, 1, keepdims=False)
        counts = lax.dynamic_index_in_dim(tile_count, region_id, 1, keepdims=False)
        occupied = slot_ids[None, :] < counts[:, None]
        masked = jnp.where(occupied[:, :, None, None], prints.astype(jnp.float32), jnp.float32(0.0))
        picked = region_block[chosen].astype(jnp.float32)
        return evolved + jnp.einsum('bsij,bsjm->bim', masked, picked)
    start = jnp.zeros((NBLK, TILE, MEMBERS), jnp.float32)
    evolved = lax.fori_loop(0, N_FLUX, one_region, start).reshape(NOBS, MEMBERS)
    mean_sim = jnp.mean(evolved, axis=1)
    scaled = (evolved - mean_sim[:, None]) / obs_sigma[:, None]
    innovation = (observed - mean_sim) / obs_sigma
    gram = jnp.dot(scaled.T, scaled, precision=lax.Precision.HIGHEST)
    proj = jnp.dot(innovation, scaled, precision=lax.Precision.HIGHEST)
    eye = jnp.eye(MEMBERS, dtype=jnp.float32)
    system = (MEMBERS - 1.0) * eye + gram
    factor = jnp.linalg.cholesky(system)
    solved = jax.scipy.linalg.cho_solve((factor, True), jnp.concatenate([proj[:, None], gram], axis=1))
    weights = eye - 0.5 * solved[:, 1:] + solved[:, 0][:, None]
    prior = ensemble.astype(jnp.float32)
    prior_mean = jnp.mean(prior, axis=1)
    anomaly = prior - prior_mean[:, None]
    posterior = prior_mean[:, None] + jnp.dot(anomaly, weights, precision=lax.Precision.HIGHEST)
    return posterior.astype(jnp.bfloat16)
```

```python
import functools

import jax
import jax.numpy as jnp
from jax import lax
from jax.experimental import pallas as pl
from jax.experimental.pallas import tpu as pltpu
from jax.sharding import Mesh
from jax.sharding import PartitionSpec as P

OBS = ("obs_0", "obs_1")
FLUX = ("flux_0", "flux_1")
OBS_FLUX = OBS + FLUX
MESH = pl.DeviceIdType.MESH
F32 = jnp.float32
BF16 = jnp.bfloat16
Z = 16
Q = 4


def update_kernel(
    index_ref, count_ref, ensemble_ref, footprint_ref, observed_ref, sigma_ref,
    gram_ref,
    region, prints, part, pair_out, pair_in, right_out, right_in, left_out, left_in,
    halves, half_in, z_out, z_in, plane_out, plane_in,
    local_sems, hop_send, hop_recv, pair_send, pair_recv,
    right_send, right_recv, left_send, left_recv, half_sems,
    z_send, z_recv, plane_send, plane_recv, share_send, share_recv, give_send, give_recv,
):
    y, x = lax.axis_index("obs_0"), lax.axis_index("obs_1")
    z, c = lax.axis_index("flux_0"), lax.axis_index("flux_1")
    other = 1 - c

    def along_z(step):
        return (y, x, lax.rem(z + step + Z, Z), c)

    def in_plane(dy, dx):
        return (lax.rem(y + dy + Q, Q), lax.rem(x + dx + Q, Q), z, c)

    def hop(first, second):
        return in_plane(c * first + other * second, other * first + c * second)

    def owner(first, second):
        at = hop(first, second)
        return at[0] * Q + at[1]

    partner = (y, x, z, other)
    mine = y * Q + x

    load_prints = pltpu.make_async_copy(footprint_ref, prints, local_sems.at[0])
    load_prints.start()
    own = pltpu.make_async_copy(ensemble_ref, region.at[pl.ds(2 * mine, 2)], local_sems.at[1])
    own.start()

    barrier = pltpu.get_barrier_semaphore()
    pl.semaphore_signal(barrier, inc=1, device_id=partner, device_id_type=MESH)

    @pl.loop(1, Z)
    def _(step):
        pl.semaphore_signal(barrier, inc=1, device_id=along_z(step), device_id_type=MESH)
        pl.semaphore_signal(
            barrier, inc=1, device_id=in_plane(step // Q, lax.rem(step, Q)), device_id_type=MESH
        )

    pl.semaphore_wait(barrier, 2 * Z - 1)

    def piece(src, dst, sem, to):
        return pltpu.make_async_remote_copy(
            src_ref=src, dst_ref=dst, send_sem=hop_send.at[sem], recv_sem=hop_recv.at[sem],
            device_id=to, device_id_type=MESH,
        )

    def arrived(ref, sem):
        piece(ref, ref, sem, partner).wait_recv()

    sent = []

    def send(src, dst, sem, to):
        copy = piece(src, dst, sem, to)
        copy.start()
        sent.append(copy)

    def rows(o):
        return region.at[pl.ds(2 * o, 2)]

    def tile(o, k):
        return region.at[2 * o + k]

    forward, back = hop(1, 0), hop(-1, 0)
    up, down = hop(0, 1), hop(0, -1)

    def rows_at(src, o, k):
        send(src, rows(o), 4 + 4 * k, up)
        send(src, rows(o), 5 + 4 * k, down)

    def pass_on(first, k):
        lower, upper = owner(first, -1), owner(first, 1)
        arrived(rows(lower), 4 + 4 * k)
        send(tile(lower, 0), tile(lower, 0), 6 + 4 * k, up)
        arrived(rows(upper), 5 + 4 * k)
        send(tile(upper, 1), tile(upper, 1), 7 + 4 * k, down)

    send(ensemble_ref, rows(mine), 0, forward)
    send(ensemble_ref, rows(mine), 1, back)
    rows_at(ensemble_ref, mine, 0)
    behind, ahead, across = owner(-1, 0), owner(1, 0), owner(2, 0)
    arrived(rows(behind), 0)
    send(tile(behind, 0), tile(behind, 0), 2, forward)
    rows_at(rows(behind), behind, 1)
    arrived(rows(ahead), 1)
    send(tile(ahead, 1), tile(ahead, 1), 3, back)
    rows_at(rows(ahead), ahead, 2)
    pass_on(0, 0)
    arrived(tile(across, 0), 2)
    arrived(tile(across, 1), 3)
    rows_at(rows(across), across, 3)
    pass_on(-1, 1)
    pass_on(1, 2)
    pass_on(2, 3)
    for k, first in enumerate((0, -1, 1, 2)):
        far = owner(first, 2)
        arrived(tile(far, 0), 6 + 4 * k)
        arrived(tile(far, 1), 7 + 4 * k)
    own.wait()
    load_prints.wait()

    def offset(t):
        s = t // 2
        return jnp.where(lax.rem(t, 2) == 0, 8 - s, 9 + s)

    def pair_copy(t):
        return pltpu.make_async_remote_copy(
            src_ref=pair_out.at[t], dst_ref=pair_in.at[t], send_sem=pair_send.at[t],
            recv_sem=pair_recv.at[t], device_id=partner, device_id_type=MESH,
        )

    def block(t):
        b = lax.rem(z + offset(t), Z)
        count = count_ref[b]
        lhs, rhs = [], []
        for s in range(8):
            values = prints[b, s]
            lhs.append(jnp.where(s < count, values, jnp.zeros_like(values)))
            at = index_ref[b, s]
            rhs.append(region[at])
        total = jnp.dot(
            jnp.concatenate(lhs, axis=1), jnp.concatenate(rhs, axis=0), preferred_element_type=F32
        )
        part[t] = jnp.where(c == 0, total[:64], total[64:])
        pair_out[t] = jnp.where(c == 0, total[64:], total[:64]).astype(BF16)
        pair_copy(t).start()

    def right_copy(s):
        return pltpu.make_async_remote_copy(
            src_ref=right_out.at[s], dst_ref=right_in.at[s + 1], send_sem=right_send.at[s],
            recv_sem=right_recv.at[s + 1], device_id=along_z(1), device_id_type=MESH,
        )

    def left_copy(s):
        return pltpu.make_async_remote_copy(
            src_ref=left_out.at[s], dst_ref=left_in.at[s + 1], send_sem=left_send.at[s],
            recv_sem=left_recv.at[s + 1], device_id=along_z(-1), device_id_type=MESH,
        )

    right_in[0] = jnp.zeros_like(right_in[0])
    left_in[0] = jnp.zeros_like(left_in[0])

    def own_sum(t):
        pair_copy(t).wait_recv()
        return part[t] + pair_in[t].astype(F32)

    @pl.loop(0, 9)
    def _(s):
        @pl.when(s < 8)
        def _():
            block(2 * s)
            block(2 * s + 1)

        @pl.when(s >= 1)
        def _():
            now = s - 1
            rightward = own_sum(2 * now)

            @pl.when(now >= 1)
            def _():
                right_copy(now - 1).wait_recv()

            right_out[now] = (rightward + right_in[now].astype(F32)).astype(BF16)
            right_copy(now).start()

            @pl.when(now < 7)
            def _():
                leftward = own_sum(2 * now + 1)

                @pl.when(now >= 1)
                def _():
                    left_copy(now - 1).wait_recv()

                left_out[now] = (leftward + left_in[now].astype(F32)).astype(BF16)
                left_copy(now).start()

    evolved = own_sum(15)
    left_copy(6).wait_recv()
    evolved = evolved + left_in[7].astype(F32)
    right_copy(7).wait_recv()
    evolved = evolved + right_in[8].astype(F32)

    lines = lax.broadcasted_iota(jnp.int32, (64, 64), 0)
    columns = lax.broadcasted_iota(jnp.int32, (64, 64), 1)

    def upright(row):
        return jnp.sum(jnp.where(lines == columns, row, 0.0), axis=1, keepdims=True)

    sigma = upright(sigma_ref[...])
    mean_sim = jnp.mean(evolved, axis=1, keepdims=True)
    scaled = (evolved - mean_sim) / sigma
    innovation = (upright(observed_ref[...]) - mean_sim) / sigma
    gram = lax.dot_general(
        scaled, scaled, (((0,), (0,)), ((), ())), precision=lax.Precision.HIGHEST,
        preferred_element_type=F32,
    )
    proj = jnp.sum(innovation * scaled, axis=0, keepdims=True)
    halves[0] = gram[:128]
    halves[1, :, :128] = gram[128:, 128:]
    line = lax.broadcasted_iota(jnp.int32, (128, 128), 0)
    halves[1, :, 128:] = jnp.where(
        line == 0, proj[:, :128], jnp.where(line == 1, proj[:, 128:], 0.0)
    )

    half_copy = pltpu.make_async_remote_copy(
        src_ref=halves.at[other], dst_ref=half_in, send_sem=half_sems.at[0],
        recv_sem=half_sems.at[1], device_id=partner, device_id_type=MESH,
    )
    half_copy.start()
    half_copy.wait_recv()
    z_out[...] = (halves[c] + half_in[...]).reshape(Z, 8, 256)

    def z_copy(t):
        step = offset(t)
        return pltpu.make_async_remote_copy(
            src_ref=z_out.at[lax.rem(z + step, Z)], dst_ref=z_in.at[t], send_sem=z_send.at[t],
            recv_sem=z_recv.at[t], device_id=along_z(step), device_id_type=MESH,
        )

    @pl.loop(0, Z - 1)
    def _(t):
        z_copy(t).start()

    def add_z(i, total):
        t = Z - 2 - i
        z_copy(t).wait_recv()
        return total + z_in[t]

    plane_out[...] = lax.fori_loop(0, Z - 1, add_z, z_out[z])

    def plane_copy(t):
        return pltpu.make_async_remote_copy(
            src_ref=plane_out, dst_ref=plane_in.at[t], send_sem=plane_send.at[t],
            recv_sem=plane_recv.at[t], device_id=in_plane(t // Q, lax.rem(t, Q)), device_id_type=MESH,
        )

    @pl.loop(1, Z)
    def _(t):
        plane_copy(t).start()

    def add_plane(t, total):
        plane_copy(t).wait_recv()
        return total + plane_in[t]

    whole = lax.fori_loop(1, Z, add_plane, plane_out[...])
    gram_ref[c, z] = whole

    def share_copy(t, at):
        return pltpu.make_async_remote_copy(
            src_ref=gram_ref.at[c, at], dst_ref=gram_ref.at[c, at], send_sem=share_send.at[t],
            recv_sem=share_recv.at[t], device_id=along_z(offset(t)), device_id_type=MESH,
        )

    def give_copy(t, half, at):
        return pltpu.make_async_remote_copy(
            src_ref=gram_ref.at[half, at], dst_ref=gram_ref.at[half, at], send_sem=give_send.at[t],
            recv_sem=give_recv.at[t], device_id=partner, device_id_type=MESH,
        )

    @pl.loop(0, Z - 1)
    def _(t):
        share_copy(t, z).start()

    give_copy(15, c, z).start()

    @pl.loop(0, Z - 1)
    def _(i):
        t = Z - 2 - i
        at = lax.rem(z - offset(t) + Z, Z)
        share_copy(t, at).wait_recv()
        give_copy(t, c, at).start()

    @pl.loop(0, Z)
    def _(i):
        t = Z - 1 - i
        at = lax.rem(z - offset(t) + Z, Z)
        give_copy(t, other, at).wait_recv()

    for copy in sent:
        copy.wait_send()
    half_copy.wait_send()

    @pl.loop(0, Z)
    def _(t):
        pair_copy(t).wait_send()
        give_copy(t, c, z).wait_send()

    @pl.loop(0, 8)
    def _(s):
        right_copy(s).wait_send()

    @pl.loop(0, 7)
    def _(s):
        left_copy(s).wait_send()

    @pl.loop(0, Z - 1)
    def _(t):
        z_copy(t).wait_send()
        plane_copy(t + 1).wait_send()
        share_copy(t, z).wait_send()


def summed_gram(ensemble, footprint, tile_index, tile_count, observed, obs_sigma):
    dma = pltpu.SemaphoreType.DMA
    vmem = pltpu.VMEM
    return pl.pallas_call(
        update_kernel,
        out_shape=jax.ShapeDtypeStruct((2, Z, 8, 256), F32),
        in_specs=[
            pl.BlockSpec(memory_space=pltpu.SMEM),
            pl.BlockSpec(memory_space=pltpu.SMEM),
            pl.BlockSpec(memory_space=pl.ANY),
            pl.BlockSpec(memory_space=pl.ANY),
            pl.BlockSpec(memory_space=vmem),
            pl.BlockSpec(memory_space=vmem),
        ],
        out_specs=pl.BlockSpec(memory_space=vmem),
        scratch_shapes=[
            vmem((32, 128, 256), BF16),
            vmem((16, 8, 128, 128), BF16),
            vmem((16, 64, 256), F32),
            vmem((16, 64, 256), BF16),
            vmem((16, 64, 256), BF16),
            vmem((8, 64, 256), BF16),
            vmem((9, 64, 256), BF16),
            vmem((7, 64, 256), BF16),
            vmem((8, 64, 256), BF16),
            vmem((2, 128, 256), F32),
            vmem((128, 256), F32),
            vmem((Z, 8, 256), F32),
            vmem((Z, 8, 256), F32),
            vmem((8, 256), F32),
            vmem((Z, 8, 256), F32),
            dma((2,)),
            dma((20,)),
            dma((20,)),
            dma((16,)),
            dma((16,)),
            dma((8,)),
            dma((9,)),
            dma((7,)),
            dma((8,)),
            dma((2,)),
            dma((Z,)),
            dma((Z,)),
            dma((Z,)),
            dma((Z,)),
            dma((Z,)),
            dma((Z,)),
            dma((Z,)),
            dma((Z,)),
        ],
        compiler_params=pltpu.CompilerParams(collective_id=0, has_side_effects=True),
    )(
        tile_index.reshape(16, 8), tile_count.reshape(16), ensemble.reshape(2, 128, 256),
        footprint.reshape(16, 8, 128, 128), observed.reshape(1, 64), obs_sigma.reshape(1, 64),
    )


def per_device(ensemble, footprint, tile_index, tile_count, observed, obs_sigma):
    members = ensemble.shape[1]
    packed = summed_gram(ensemble, footprint, tile_index, tile_count, observed, obs_sigma)
    packed = packed.reshape(2, 128, 256)
    top, corner = packed[0], packed[1, :, :128]
    proj = packed[1, :2, 128:].reshape(256)
    gram = jnp.concatenate([top, jnp.concatenate([top[:, 128:].T, corner], axis=1)], axis=0)
    eye = jnp.eye(members, dtype=jnp.float32)
    system = (members - 1.0) * eye + gram
    factor = jnp.linalg.cholesky(system)
    solved = jax.scipy.linalg.cho_solve(
        (factor, True), jnp.concatenate([proj[:, None], gram], axis=1)
    )
    weights = eye - 0.5 * solved[:, 1:] + solved[:, 0][:, None]
    prior = ensemble.astype(jnp.float32)
    prior_mean = jnp.mean(prior, axis=1)
    anomaly = prior - prior_mean[:, None]
    posterior = prior_mean[:, None] + jnp.dot(anomaly, weights, precision=lax.Precision.HIGHEST)
    return posterior.astype(jnp.bfloat16)


def solution(mesh):
    finer = Mesh(mesh.devices.reshape(4, 4, 16, 2), OBS_FLUX)
    placed = (
        P(OBS_FLUX, None),
        P(OBS, FLUX, None, None, None),
        P(OBS, FLUX, None),
        P(OBS, FLUX),
        P(OBS_FLUX),
        P(OBS_FLUX),
    )
    return jax.shard_map(
        per_device, mesh=finer, in_specs=placed, out_specs=P(OBS_FLUX, None), check_vma=False
    )
```

```python
import jax
import jax.numpy as jnp
from jax import lax
from jax.experimental import pallas as pl
from jax.experimental.pallas import tpu as pltpu
from jax.sharding import Mesh
from jax.sharding import PartitionSpec as P

OBS = ("obs_0", "obs_1")
FLUX = ("flux_0", "flux_1")
OBS_FLUX = OBS + FLUX
HIGH = lax.Precision.HIGHEST
MESH = pl.DeviceIdType.MESH
F32 = jnp.float32
BF16 = jnp.bfloat16
Z = 16
Q = 4


def update_kernel(
    index_ref, count_ref, ensemble_ref, footprint_ref, observed_ref, sigma_ref,
    gram_ref,
    region, prints, part, pair_out, pair_in, right_out, right_in, left_out, left_in,
    halves, half_in, z_out, z_in, plane_out, plane_in,
    local_sems, hop_send, hop_recv, pair_send, pair_recv,
    right_send, right_recv, left_send, left_recv, half_sems,
    z_send, z_recv, plane_send, plane_recv, share_send, share_recv, give_send, give_recv,
):
    y, x = lax.axis_index("obs_0"), lax.axis_index("obs_1")
    z, c = lax.axis_index("flux_0"), lax.axis_index("flux_1")
    other = 1 - c

    def along_z(step):
        return (y, x, lax.rem(z + step + Z, Z), c)

    def in_plane(dy, dx):
        return (lax.rem(y + dy + Q, Q), lax.rem(x + dx + Q, Q), z, c)

    def hop(first, second):
        return in_plane(c * first + other * second, other * first + c * second)

    def owner(first, second):
        at = hop(first, second)
        return at[0] * Q + at[1]

    partner = (y, x, z, other)
    mine = y * Q + x

    load_prints = pltpu.make_async_copy(footprint_ref, prints, local_sems.at[0])
    load_prints.start()
    own = pltpu.make_async_copy(ensemble_ref, region.at[pl.ds(2 * mine, 2)], local_sems.at[1])
    own.start()

    barrier = pltpu.get_barrier_semaphore()
    pl.semaphore_signal(barrier, inc=1, device_id=partner, device_id_type=MESH)

    @pl.loop(1, Z)
    def _(step):
        pl.semaphore_signal(barrier, inc=1, device_id=along_z(step), device_id_type=MESH)
        pl.semaphore_signal(
            barrier, inc=1, device_id=in_plane(step // Q, lax.rem(step, Q)), device_id_type=MESH
        )

    pl.semaphore_wait(barrier, 2 * Z - 1)

    def piece(src, dst, sem, to):
        return pltpu.make_async_remote_copy(
            src_ref=src, dst_ref=dst, send_sem=hop_send.at[sem], recv_sem=hop_recv.at[sem],
            device_id=to, device_id_type=MESH,
        )

    def arrived(ref, sem):
        piece(ref, ref, sem, partner).wait_recv()

    sent = []

    def send(src, dst, sem, to):
        copy = piece(src, dst, sem, to)
        copy.start()
        sent.append(copy)

    def rows(o):
        return region.at[pl.ds(2 * o, 2)]

    def tile(o, k):
        return region.at[2 * o + k]

    forward, back = hop(1, 0), hop(-1, 0)
    up, down = hop(0, 1), hop(0, -1)

    def rows_at(src, o, k):
        send(src, rows(o), 4 + 4 * k, up)
        send(src, rows(o), 5 + 4 * k, down)

    def pass_on(first, k):
        lower, upper = owner(first, -1), owner(first, 1)
        arrived(rows(lower), 4 + 4 * k)
        send(tile(lower, 0), tile(lower, 0), 6 + 4 * k, up)
        arrived(rows(upper), 5 + 4 * k)
        send(tile(upper, 1), tile(upper, 1), 7 + 4 * k, down)

    send(ensemble_ref, rows(mine), 0, forward)
    send(ensemble_ref, rows(mine), 1, back)
    rows_at(ensemble_ref, mine, 0)
    behind, ahead, across = owner(-1, 0), owner(1, 0), owner(2, 0)
    arrived(rows(behind), 0)
    send(tile(behind, 0), tile(behind, 0), 2, forward)
    rows_at(rows(behind), behind, 1)
    arrived(rows(ahead), 1)
    send(tile(ahead, 1), tile(ahead, 1), 3, back)
    rows_at(rows(ahead), ahead, 2)
    pass_on(0, 0)
    arrived(tile(across, 0), 2)
    arrived(tile(across, 1), 3)
    rows_at(rows(across), across, 3)
    pass_on(-1, 1)
    pass_on(1, 2)
    pass_on(2, 3)
    for k, first in enumerate((0, -1, 1, 2)):
        far = owner(first, 2)
        arrived(tile(far, 0), 6 + 4 * k)
        arrived(tile(far, 1), 7 + 4 * k)
    own.wait()
    load_prints.wait()

    def offset(t):
        s = t // 2
        return jnp.where(lax.rem(t, 2) == 0, 8 - s, 9 + s)

    def pair_copy(t):
        return pltpu.make_async_remote_copy(
            src_ref=pair_out.at[t], dst_ref=pair_in.at[t], send_sem=pair_send.at[t],
            recv_sem=pair_recv.at[t], device_id=partner, device_id_type=MESH,
        )

    def block(t):
        b = lax.rem(z + offset(t), Z)
        count = count_ref[b]
        lhs, rhs = [], []
        for s in range(8):
            values = prints[b, s]
            lhs.append(jnp.where(s < count, values, jnp.zeros_like(values)))
            at = index_ref[b, s]
            rhs.append(region[at])
        total = jnp.dot(
            jnp.concatenate(lhs, axis=1), jnp.concatenate(rhs, axis=0), preferred_element_type=F32
        )
        part[t] = jnp.where(c == 0, total[:64], total[64:])
        pair_out[t] = jnp.where(c == 0, total[64:], total[:64]).astype(BF16)
        pair_copy(t).start()

    def right_copy(s):
        return pltpu.make_async_remote_copy(
            src_ref=right_out.at[s], dst_ref=right_in.at[s + 1], send_sem=right_send.at[s],
            recv_sem=right_recv.at[s + 1], device_id=along_z(1), device_id_type=MESH,
        )

    def left_copy(s):
        return pltpu.make_async_remote_copy(
            src_ref=left_out.at[s], dst_ref=left_in.at[s + 1], send_sem=left_send.at[s],
            recv_sem=left_recv.at[s + 1], device_id=along_z(-1), device_id_type=MESH,
        )

    right_in[0] = jnp.zeros_like(right_in[0])
    left_in[0] = jnp.zeros_like(left_in[0])

    def own_sum(t):
        pair_copy(t).wait_recv()
        return part[t] + pair_in[t].astype(F32)

    @pl.loop(0, 9)
    def _(s):
        @pl.when(s < 8)
        def _():
            block(2 * s)
            block(2 * s + 1)

        @pl.when(s >= 1)
        def _():
            now = s - 1
            rightward = own_sum(2 * now)

            @pl.when(now >= 1)
            def _():
                right_copy(now - 1).wait_recv()

            right_out[now] = (rightward + right_in[now].astype(F32)).astype(BF16)
            right_copy(now).start()

            @pl.when(now < 7)
            def _():
                leftward = own_sum(2 * now + 1)

                @pl.when(now >= 1)
                def _():
                    left_copy(now - 1).wait_recv()

                left_out[now] = (leftward + left_in[now].astype(F32)).astype(BF16)
                left_copy(now).start()

    evolved = own_sum(15)
    left_copy(6).wait_recv()
    evolved = evolved + left_in[7].astype(F32)
    right_copy(7).wait_recv()
    evolved = evolved + right_in[8].astype(F32)

    lines = lax.broadcasted_iota(jnp.int32, (64, 64), 0)
    columns = lax.broadcasted_iota(jnp.int32, (64, 64), 1)

    def upright(row):
        return jnp.sum(jnp.where(lines == columns, row, 0.0), axis=1, keepdims=True)

    sigma = upright(sigma_ref[...])
    mean_sim = jnp.mean(evolved, axis=1, keepdims=True)
    scaled = (evolved - mean_sim) / sigma
    innovation = (upright(observed_ref[...]) - mean_sim) / sigma
    gram = lax.dot_general(
        scaled, scaled, (((0,), (0,)), ((), ())), precision=HIGH,
        preferred_element_type=F32,
    )
    proj = jnp.sum(innovation * scaled, axis=0, keepdims=True)
    halves[0] = gram[:128]
    halves[1, :, :128] = gram[128:, 128:]
    line = lax.broadcasted_iota(jnp.int32, (128, 128), 0)
    halves[1, :, 128:] = jnp.where(
        line == 0, proj[:, :128], jnp.where(line == 1, proj[:, 128:], 0.0)
    )

    half_copy = pltpu.make_async_remote_copy(
        src_ref=halves.at[other], dst_ref=half_in, send_sem=half_sems.at[0],
        recv_sem=half_sems.at[1], device_id=partner, device_id_type=MESH,
    )
    half_copy.start()
    half_copy.wait_recv()
    z_out[...] = (halves[c] + half_in[...]).reshape(Z, 8, 256)

    def z_copy(t):
        step = offset(t)
        return pltpu.make_async_remote_copy(
            src_ref=z_out.at[lax.rem(z + step, Z)], dst_ref=z_in.at[t], send_sem=z_send.at[t],
            recv_sem=z_recv.at[t], device_id=along_z(step), device_id_type=MESH,
        )

    @pl.loop(0, Z - 1)
    def _(t):
        z_copy(t).start()

    def add_z(i, total):
        t = Z - 2 - i
        z_copy(t).wait_recv()
        return total + z_in[t]

    plane_out[...] = lax.fori_loop(0, Z - 1, add_z, z_out[z])

    def plane_copy(t):
        return pltpu.make_async_remote_copy(
            src_ref=plane_out, dst_ref=plane_in.at[t], send_sem=plane_send.at[t],
            recv_sem=plane_recv.at[t], device_id=in_plane(t // Q, lax.rem(t, Q)), device_id_type=MESH,
        )

    @pl.loop(1, Z)
    def _(t):
        plane_copy(t).start()

    def add_plane(t, total):
        plane_copy(t).wait_recv()
        return total + plane_in[t]

    whole = lax.fori_loop(1, Z, add_plane, plane_out[...])
    gram_ref[c, z] = whole

    def share_copy(t, at):
        return pltpu.make_async_remote_copy(
            src_ref=gram_ref.at[c, at], dst_ref=gram_ref.at[c, at], send_sem=share_send.at[t],
            recv_sem=share_recv.at[t], device_id=along_z(offset(t)), device_id_type=MESH,
        )

    def give_copy(t, half, at):
        return pltpu.make_async_remote_copy(
            src_ref=gram_ref.at[half, at], dst_ref=gram_ref.at[half, at], send_sem=give_send.at[t],
            recv_sem=give_recv.at[t], device_id=partner, device_id_type=MESH,
        )

    @pl.loop(0, Z - 1)
    def _(t):
        share_copy(t, z).start()

    give_copy(15, c, z).start()

    @pl.loop(0, Z - 1)
    def _(i):
        t = Z - 2 - i
        at = lax.rem(z - offset(t) + Z, Z)
        share_copy(t, at).wait_recv()
        give_copy(t, c, at).start()

    @pl.loop(0, Z)
    def _(i):
        t = Z - 1 - i
        at = lax.rem(z - offset(t) + Z, Z)
        give_copy(t, other, at).wait_recv()

    for copy in sent:
        copy.wait_send()
    half_copy.wait_send()

    @pl.loop(0, Z)
    def _(t):
        pair_copy(t).wait_send()
        give_copy(t, c, z).wait_send()

    @pl.loop(0, 8)
    def _(s):
        right_copy(s).wait_send()

    @pl.loop(0, 7)
    def _(s):
        left_copy(s).wait_send()

    @pl.loop(0, Z - 1)
    def _(t):
        z_copy(t).wait_send()
        plane_copy(t + 1).wait_send()
        share_copy(t, z).wait_send()


def summed_gram(ensemble, footprint, tile_index, tile_count, observed, obs_sigma):
    dma = pltpu.SemaphoreType.DMA
    vmem = pltpu.VMEM
    return pl.pallas_call(
        update_kernel,
        out_shape=jax.ShapeDtypeStruct((2, Z, 8, 256), F32),
        in_specs=[
            pl.BlockSpec(memory_space=pltpu.SMEM),
            pl.BlockSpec(memory_space=pltpu.SMEM),
            pl.BlockSpec(memory_space=pl.ANY),
            pl.BlockSpec(memory_space=pl.ANY),
            pl.BlockSpec(memory_space=vmem),
            pl.BlockSpec(memory_space=vmem),
        ],
        out_specs=pl.BlockSpec(memory_space=vmem),
        scratch_shapes=[
            vmem((32, 128, 256), BF16),
            vmem((16, 8, 128, 128), BF16),
            vmem((16, 64, 256), F32),
            vmem((16, 64, 256), BF16),
            vmem((16, 64, 256), BF16),
            vmem((8, 64, 256), BF16),
            vmem((9, 64, 256), BF16),
            vmem((7, 64, 256), BF16),
            vmem((8, 64, 256), BF16),
            vmem((2, 128, 256), F32),
            vmem((128, 256), F32),
            vmem((Z, 8, 256), F32),
            vmem((Z, 8, 256), F32),
            vmem((8, 256), F32),
            vmem((Z, 8, 256), F32),
            dma((2,)),
            dma((20,)),
            dma((20,)),
            dma((16,)),
            dma((16,)),
            dma((8,)),
            dma((9,)),
            dma((7,)),
            dma((8,)),
            dma((2,)),
            dma((Z,)),
            dma((Z,)),
            dma((Z,)),
            dma((Z,)),
            dma((Z,)),
            dma((Z,)),
            dma((Z,)),
            dma((Z,)),
        ],
        compiler_params=pltpu.CompilerParams(collective_id=0, has_side_effects=True),
    )(
        tile_index.reshape(16, 8), tile_count.reshape(16), ensemble.reshape(2, 128, 256),
        footprint.reshape(16, 8, 128, 128), observed.reshape(1, 64), obs_sigma.reshape(1, 64),
    )


def small_inverse(s):
    n = len(s)
    if n == 1:
        return [[1.0 / s[0][0]]]
    if n == 2:
        scale = 1.0 / (s[0][0] * s[1][1] - s[0][1] * s[0][1])
        off = -s[0][1] * scale
        return [[s[1][1] * scale, off], [off, s[0][0] * scale]]
    h = n // 2
    low, high = range(h), range(h, n)
    e = small_inverse([[s[i][j] for j in low] for i in low])
    ef = [[sum(e[i][k] * s[k][j] for k in low) for j in high] for i in low]
    rest = [[s[i][j] - sum(s[k][i] * ef[k][j - h] for k in low) for j in high] for i in high]
    r = small_inverse(rest)
    off = [[-sum(ef[i][k] * r[k][j] for k in range(n - h)) for j in range(n - h)] for i in low]
    top = [[e[i][j] - sum(off[i][k] * ef[j][k] for k in range(n - h)) for j in low] for i in low]
    out = [[None] * n for _ in range(n)]
    for i in range(n):
        for j in range(n):
            a, b = min(i, j), max(i, j)
            out[i][j] = top[a][b] if b < h else (off[a][b - h] if a < h else r[a - h][b - h])
    return out


def eliminate(panel, first, m):
    rows, lanes = panel.shape
    line = lax.broadcasted_iota(jnp.int32, (rows, 128), 0)
    column = lax.broadcasted_iota(jnp.int32, (rows, 128), 1)
    tiles = [panel[:, 128 * t : 128 * t + 128] for t in range(lanes // 128)]
    home, base = first // 128, first % 128
    for g in range(0, rows, m):
        spread = [
            jnp.broadcast_to(tiles[home][:, base + g + a : base + g + a + 1], (rows, 128)) for a in range(m)
        ]
        small = [[spread[b][g + a : g + a + 1] for b in range(m)] for a in range(m)]
        inverse = small_inverse(small)
        picked = [[tile[g + a : g + a + 1] for a in range(m)] for tile in tiles]
        here = column[:1]
        for a in range(m):
            at = base + g + a
            for b in range(m):
                picked[home][b] = jnp.where(here == at, 1.0 if a == b else 0.0, picked[home][b])
            tiles[home] = jnp.where(column == at, 0.0, tiles[home])
        for t in range(len(tiles)):
            new = [sum(inverse[a][b] * picked[t][b] for b in range(m)) for a in range(m)]
            value = tiles[t]
            for a in range(m):
                value = value - spread[a] * new[a]
            for a in range(m):
                value = jnp.where(line == g + a, new[a], value)
            tiles[t] = value
    return jnp.concatenate(tiles, axis=1)


def posterior_kernel(gram_ref, ensemble_ref, out_ref, full, stack):
    n, b, m = 256, 64, 4
    packed_top = gram_ref[0]
    corner = gram_ref[1]
    line = lax.broadcasted_iota(jnp.int32, (128, 128), 0)
    column = lax.broadcasted_iota(jnp.int32, (128, 128), 1)
    shift = jnp.where(line == column, n - 1.0, 0.0)
    full[:128, :128] = packed_top[:, :128] + shift
    full[:128, 128:] = packed_top[:, 128:]
    full[128:, :128] = packed_top[:, 128:].T
    full[128:, 128:] = corner[:, :128] + shift
    proj = jnp.concatenate([corner[:1, 128:], corner[1:2, 128:]], axis=1)
    lanes = lax.broadcasted_iota(jnp.int32, (n, n), 1)
    stack[...] = jnp.zeros_like(stack)
    for k in range(0, n, b):
        solved = eliminate(full[k : k + b, :], k, m)
        home, base = k // 128 * 128, k % 128
        if base == 0:
            stack[...] = jnp.zeros_like(stack)
        elif k:
            stack[base - b : base] = jnp.zeros((b, n), F32)
        stack[base : base + b] = solved
        change = jnp.dot(full[:, home : home + 128], stack[...], precision=HIGH, preferred_element_type=F32)
        full[...] = jnp.where((lanes >= k) & (lanes < k + b), 0.0, full[...]) - change
        full[k : k + b] = solved
    inverse = full[...]
    mean_weights = jnp.sum(inverse * proj, axis=1, keepdims=True)
    rows = lax.broadcasted_iota(jnp.int32, (n, n), 0)
    weights = 0.5 * (n - 1.0) * inverse + jnp.where(rows == lanes, 0.5, 0.0) + mean_weights
    prior = ensemble_ref[...].astype(F32)
    prior_mean = jnp.mean(prior, axis=1, keepdims=True)
    moved = jnp.dot(prior - prior_mean, weights, precision=HIGH, preferred_element_type=F32)
    out_ref[...] = (prior_mean + moved).astype(BF16)


def per_device(ensemble, footprint, tile_index, tile_count, observed, obs_sigma):
    packed = summed_gram(ensemble, footprint, tile_index, tile_count, observed, obs_sigma)
    vmem = pl.BlockSpec(memory_space=pltpu.VMEM)
    return pl.pallas_call(
        posterior_kernel,
        out_shape=jax.ShapeDtypeStruct((256, 256), BF16),
        in_specs=[vmem, vmem],
        out_specs=vmem,
        scratch_shapes=[pltpu.VMEM((256, 256), F32), pltpu.VMEM((128, 256), F32)],
    )(packed.reshape(2, 128, 256), ensemble)


def solution(mesh):
    finer = Mesh(mesh.devices.reshape(4, 4, 16, 2), OBS_FLUX)
    placed = (
        P(OBS_FLUX, None),
        P(OBS, FLUX, None, None, None),
        P(OBS, FLUX, None),
        P(OBS, FLUX),
        P(OBS_FLUX),
        P(OBS_FLUX),
    )
    return jax.shard_map(
        per_device, mesh=finer, in_specs=placed, out_specs=P(OBS_FLUX, None), check_vma=False
    )
```

```python
import jax
import jax.numpy as jnp
from jax import lax
from jax.experimental import pallas as pl
from jax.experimental.pallas import tpu as pltpu
from jax.sharding import Mesh
from jax.sharding import PartitionSpec as P

OBS = ("obs_0", "obs_1")
FLUX = ("flux_0", "flux_1")
OBS_FLUX = OBS + FLUX
HIGH = lax.Precision.HIGHEST
MESH = pl.DeviceIdType.MESH
F32 = jnp.float32
BF16 = jnp.bfloat16
Z = 16
Q = 4


def update_kernel(
    index_ref, count_ref, ensemble_ref, footprint_ref, observed_ref, sigma_ref,
    gram_ref,
    region, prints, part, pair_out, pair_in,
    near_right_out, near_right_in, near_left_out, near_left_in, right_out, right_in, left_out, left_in,
    halves, half_in, pieces, pieces_in, z_out, z_in,
    local_sems, hop_send, hop_recv, pair_send, pair_recv, hop_z_send, hop_z_recv, half_sems,
    scatter_send, scatter_recv, z_send, z_recv, share_send, share_recv, give_send, give_recv,
):
    y, x = lax.axis_index("obs_0"), lax.axis_index("obs_1")
    z, c = lax.axis_index("flux_0"), lax.axis_index("flux_1")
    other = 1 - c

    def along_z(step):
        return (y, x, lax.rem(z + step + Z, Z), c)

    def in_plane(dy, dx):
        return (lax.rem(y + dy + Q, Q), lax.rem(x + dx + Q, Q), z, c)

    def hop(first, second):
        return in_plane(c * first + other * second, other * first + c * second)

    def owner(first, second):
        at = hop(first, second)
        return at[0] * Q + at[1]

    partner = (y, x, z, other)
    mine = y * Q + x

    load_prints = pltpu.make_async_copy(footprint_ref, prints, local_sems.at[0])
    load_prints.start()
    own = pltpu.make_async_copy(ensemble_ref, region.at[pl.ds(2 * mine, 2)], local_sems.at[1])
    own.start()

    barrier = pltpu.get_barrier_semaphore()
    pl.semaphore_signal(barrier, inc=1, device_id=partner, device_id_type=MESH)

    @pl.loop(1, Z)
    def _(step):
        pl.semaphore_signal(barrier, inc=1, device_id=along_z(step), device_id_type=MESH)
        pl.semaphore_signal(
            barrier, inc=1, device_id=in_plane(step // Q, lax.rem(step, Q)), device_id_type=MESH
        )

    pl.semaphore_wait(barrier, 2 * Z - 1)

    def piece(src, dst, sem, to):
        return pltpu.make_async_remote_copy(
            src_ref=src, dst_ref=dst, send_sem=hop_send.at[sem], recv_sem=hop_recv.at[sem],
            device_id=to, device_id_type=MESH,
        )

    def arrived(ref, sem):
        piece(ref, ref, sem, partner).wait_recv()

    sent = []

    def send(src, dst, sem, to):
        copy = piece(src, dst, sem, to)
        copy.start()
        sent.append(copy)

    def rows(o):
        return region.at[pl.ds(2 * o, 2)]

    def tile(o, k):
        return region.at[2 * o + k]

    forward, back = hop(1, 0), hop(-1, 0)
    up, down = hop(0, 1), hop(0, -1)

    def rows_at(src, o, k):
        send(src, rows(o), 4 + 4 * k, up)
        send(src, rows(o), 5 + 4 * k, down)

    def pass_on(first, k):
        lower, upper = owner(first, -1), owner(first, 1)
        arrived(rows(lower), 4 + 4 * k)
        send(tile(lower, 0), tile(lower, 0), 6 + 4 * k, up)
        arrived(rows(upper), 5 + 4 * k)
        send(tile(upper, 1), tile(upper, 1), 7 + 4 * k, down)

    send(ensemble_ref, rows(mine), 0, forward)
    send(ensemble_ref, rows(mine), 1, back)
    rows_at(ensemble_ref, mine, 0)
    behind, ahead, across = owner(-1, 0), owner(1, 0), owner(2, 0)
    arrived(rows(behind), 0)
    send(tile(behind, 0), tile(behind, 0), 2, forward)
    rows_at(rows(behind), behind, 1)
    arrived(rows(ahead), 1)
    send(tile(ahead, 1), tile(ahead, 1), 3, back)
    rows_at(rows(ahead), ahead, 2)
    pass_on(0, 0)
    arrived(tile(across, 0), 2)
    arrived(tile(across, 1), 3)
    rows_at(rows(across), across, 3)
    pass_on(-1, 1)
    pass_on(1, 2)
    pass_on(2, 3)
    for k, first in enumerate((0, -1, 1, 2)):
        far = owner(first, 2)
        arrived(tile(far, 0), 6 + 4 * k)
        arrived(tile(far, 1), 7 + 4 * k)
    own.wait()
    load_prints.wait()

    def pair_copy(t):
        return pltpu.make_async_remote_copy(
            src_ref=pair_out.at[t], dst_ref=pair_in.at[t], send_sem=pair_send.at[t],
            recv_sem=pair_recv.at[t], device_id=partner, device_id_type=MESH,
        )

    def block(t, away):
        b = lax.rem(z + away + Z, Z)
        count = count_ref[b]
        lhs, rhs = [], []
        for s in range(8):
            values = prints[b, s]
            lhs.append(jnp.where(s < count, values, jnp.zeros_like(values)))
            rhs.append(region[index_ref[s, b]])
        total = jnp.dot(
            jnp.concatenate(lhs, axis=1), jnp.concatenate(rhs, axis=0), preferred_element_type=F32
        )
        part[t] = jnp.where(c == 0, total[:64], total[64:])
        pair_out[t] = jnp.where(c == 0, total[64:], total[:64]).astype(BF16)
        pair_copy(t).start()

    def z_hop(src, dst, k, i, step):
        return pltpu.make_async_remote_copy(
            src_ref=src.at[i], dst_ref=dst.at[i], send_sem=hop_z_send.at[k, i],
            recv_sem=hop_z_recv.at[k, i], device_id=along_z(step), device_id_type=MESH,
        )

    def near_right(i):
        return z_hop(near_right_out, near_right_in, 0, i, 1)

    def near_left(i):
        return z_hop(near_left_out, near_left_in, 1, i, -1)

    def right_copy(i):
        return z_hop(right_out, right_in, 2, i, 2 - i // 3)

    def left_copy(i):
        return z_hop(left_out, left_in, 3, i, i // 3 - 2)

    def own_sum(t):
        pair_copy(t).wait_recv()
        return part[t] + pair_in[t].astype(F32)

    @pl.loop(0, 5)
    def _(i):
        @pl.when(i < 4)
        def _():
            block(4 * i, 8 - 2 * i)
            block(4 * i + 1, 7 - 2 * i)
            block(4 * i + 2, 2 * i - 7)
            block(4 * i + 3, 2 * i - 6)
            near_right_out[i] = own_sum(4 * i).astype(BF16)
            near_right(i).start()

        @pl.when(i < 3)
        def _():
            near_left_out[i] = own_sum(4 * i + 3).astype(BF16)
            near_left(i).start()

        @pl.when(i >= 1)
        def _():
            n = i - 1
            left = own_sum(4 * n + 2)
            right = own_sum(4 * n + 1)

            @pl.when(n == 0)
            def _():
                left_out[0] = left.astype(BF16)

            @pl.when(n >= 1)
            def _():
                near_left(n - 1).wait_recv()
                left_copy(n - 1).wait_recv()
                left_out[n] = (
                    left + near_left_in[n - 1].astype(F32) + left_in[n - 1].astype(F32)
                ).astype(BF16)

            left_copy(n).start()
            near_right(n).wait_recv()
            right = right + near_right_in[n].astype(F32)

            @pl.when(n == 0)
            def _():
                right_out[0] = right.astype(BF16)

            @pl.when(n >= 1)
            def _():
                right_copy(n - 1).wait_recv()
                right_out[n] = (right + right_in[n - 1].astype(F32)).astype(BF16)

            right_copy(n).start()

    evolved = own_sum(15)
    left_copy(3).wait_recv()
    evolved = evolved + left_in[3].astype(F32)
    right_copy(3).wait_recv()
    evolved = evolved + right_in[3].astype(F32)

    lines = lax.broadcasted_iota(jnp.int32, (64, 64), 0)
    columns = lax.broadcasted_iota(jnp.int32, (64, 64), 1)

    def upright(row):
        return jnp.sum(jnp.where(lines == columns, row, 0.0), axis=1, keepdims=True)

    sigma = upright(sigma_ref[...])
    mean_sim = jnp.mean(evolved, axis=1, keepdims=True)
    scaled = (evolved - mean_sim) / sigma
    innovation = (upright(observed_ref[...]) - mean_sim) / sigma
    gram = lax.dot_general(
        scaled, scaled, (((0,), (0,)), ((), ())), precision=HIGH,
        preferred_element_type=F32,
    )
    proj = jnp.sum(innovation * scaled, axis=0, keepdims=True)
    halves[0] = gram[:128]
    halves[1, :, :128] = gram[128:, 128:]
    line = lax.broadcasted_iota(jnp.int32, (128, 128), 0)
    halves[1, :, 128:] = jnp.where(
        line == 0, proj[:, :128], jnp.where(line == 1, proj[:, 128:], 0.0)
    )

    half_copy = pltpu.make_async_remote_copy(
        src_ref=halves.at[other], dst_ref=half_in, send_sem=half_sems.at[0],
        recv_sem=half_sems.at[1], device_id=partner, device_id_type=MESH,
    )
    half_copy.start()
    half_copy.wait_recv()
    pieces[...] = (halves[c] + half_in[...]).reshape(16, 8, 256)
    plane = ((2, 2), (1, 2), (3, 2), (2, 1), (2, 3), (0, 2), (2, 0), (1, 1), (1, 3), (3, 1), (3, 3),
             (0, 1), (0, 3), (1, 0), (3, 0))

    def spot(dy, dx):
        at = in_plane(dy, dx)
        return at[0] * Q + at[1]

    def scatter_copy(t):
        return pltpu.make_async_remote_copy(
            src_ref=pieces.at[spot(*plane[t])], dst_ref=pieces_in.at[t], send_sem=scatter_send.at[t],
            recv_sem=scatter_recv.at[t], device_id=in_plane(*plane[t]), device_id_type=MESH,
        )

    for t in range(15):
        scatter_copy(t).start()
    summed = pieces[mine]
    for t in reversed(range(15)):
        scatter_copy(t).wait_recv()
        summed = summed + pieces_in[t]
    z_out[...] = summed

    def z_copy(t):
        step = jnp.where(lax.rem(t, 2) == 0, 8 - t // 2, 9 + t // 2)
        return pltpu.make_async_remote_copy(
            src_ref=z_out, dst_ref=z_in.at[t], send_sem=z_send.at[t],
            recv_sem=z_recv.at[t], device_id=along_z(step), device_id_type=MESH,
        )

    @pl.loop(0, Z - 1)
    def _(t):
        z_copy(t).start()

    def add_z(i, total):
        t = Z - 2 - i
        z_copy(t).wait_recv()
        return total + z_in[t]

    gram_ref[c, mine] = lax.fori_loop(0, Z - 1, add_z, summed)

    def share_copy(t, at):
        return pltpu.make_async_remote_copy(
            src_ref=gram_ref.at[c, at], dst_ref=gram_ref.at[c, at], send_sem=share_send.at[t],
            recv_sem=share_recv.at[t], device_id=in_plane(*plane[t]), device_id_type=MESH,
        )

    def give_copy(t, half, at):
        return pltpu.make_async_remote_copy(
            src_ref=gram_ref.at[half, at], dst_ref=gram_ref.at[half, at], send_sem=give_send.at[t],
            recv_sem=give_recv.at[t], device_id=partner, device_id_type=MESH,
        )

    def origin(t):
        dy, dx = plane[t]
        return spot(-dy, -dx)

    for t in range(15):
        share_copy(t, mine).start()
    give_copy(15, c, mine).start()
    for t in reversed(range(15)):
        share_copy(t, origin(t)).wait_recv()
        give_copy(t, c, origin(t)).start()
    give_copy(15, other, mine).wait_recv()
    for t in reversed(range(15)):
        give_copy(t, other, origin(t)).wait_recv()

    for copy in sent:
        copy.wait_send()
    half_copy.wait_send()

    @pl.loop(0, 16)
    def _(t):
        pair_copy(t).wait_send()
        give_copy(t, c, mine).wait_send()

    @pl.loop(0, 4)
    def _(i):
        near_right(i).wait_send()
        right_copy(i).wait_send()
        left_copy(i).wait_send()

    @pl.loop(0, 3)
    def _(i):
        near_left(i).wait_send()

    @pl.loop(0, Z - 1)
    def _(t):
        z_copy(t).wait_send()

    for t in range(15):
        scatter_copy(t).wait_send()
        share_copy(t, mine).wait_send()


def summed_gram(ensemble, footprint, tile_index, tile_count, observed, obs_sigma):
    dma = pltpu.SemaphoreType.DMA
    vmem = pltpu.VMEM
    return pl.pallas_call(
        update_kernel,
        out_shape=jax.ShapeDtypeStruct((2, Z, 8, 256), F32),
        in_specs=[
            pl.BlockSpec(memory_space=pltpu.SMEM),
            pl.BlockSpec(memory_space=pltpu.SMEM),
            pl.BlockSpec(memory_space=pl.ANY),
            pl.BlockSpec(memory_space=pl.ANY),
            pl.BlockSpec(memory_space=vmem),
            pl.BlockSpec(memory_space=vmem),
        ],
        out_specs=pl.BlockSpec(memory_space=vmem),
        scratch_shapes=[
            vmem((32, 128, 256), BF16),
            vmem((16, 8, 128, 128), BF16),
            vmem((16, 64, 256), F32),
            vmem((16, 64, 256), BF16),
            vmem((16, 64, 256), BF16),
            *[vmem((4, 64, 256), BF16)] * 8,
            vmem((2, 128, 256), F32),
            vmem((128, 256), F32),
            vmem((16, 8, 256), F32),
            vmem((15, 8, 256), F32),
            vmem((8, 256), F32),
            vmem((15, 8, 256), F32),
            dma((2,)),
            dma((20,)),
            dma((20,)),
            dma((16,)),
            dma((16,)),
            dma((4, 4)),
            dma((4, 4)),
            dma((2,)),
            *[dma((15,))] * 6,
            dma((16,)),
            dma((16,)),
        ],
        compiler_params=pltpu.CompilerParams(collective_id=0, has_side_effects=True),
    )(
        tile_index.reshape(16, 8).T, tile_count.reshape(16), ensemble.reshape(2, 128, 256),
        footprint.reshape(16, 8, 128, 128), observed.reshape(1, 64), obs_sigma.reshape(1, 64),
    )


def small_inverse(s):
    n = len(s)
    if n == 1:
        return [[1.0 / s[0][0]]]
    if n == 2:
        scale = 1.0 / (s[0][0] * s[1][1] - s[0][1] * s[0][1])
        off = -s[0][1] * scale
        return [[s[1][1] * scale, off], [off, s[0][0] * scale]]
    h = n // 2
    low, high = range(h), range(h, n)
    e = small_inverse([[s[i][j] for j in low] for i in low])
    ef = [[sum(e[i][k] * s[k][j] for k in low) for j in high] for i in low]
    rest = [[s[i][j] - sum(s[k][i] * ef[k][j - h] for k in low) for j in high] for i in high]
    r = small_inverse(rest)
    off = [[-sum(ef[i][k] * r[k][j] for k in range(n - h)) for j in range(n - h)] for i in low]
    top = [[e[i][j] - sum(off[i][k] * ef[j][k] for k in range(n - h)) for j in low] for i in low]
    out = [[None] * n for _ in range(n)]
    for i in range(n):
        for j in range(n):
            a, b = min(i, j), max(i, j)
            out[i][j] = top[a][b] if b < h else (off[a][b - h] if a < h else r[a - h][b - h])
    return out


def eliminate(panel, first, m):
    rows, lanes = panel.shape
    line = lax.broadcasted_iota(jnp.int32, (rows, 128), 0)
    column = lax.broadcasted_iota(jnp.int32, (rows, 128), 1)
    tiles = [panel[:, 128 * t : 128 * t + 128] for t in range(lanes // 128)]
    home, base = first // 128, first % 128
    for g in range(0, rows, m):
        spread = [
            jnp.broadcast_to(tiles[home][:, base + g + a : base + g + a + 1], (rows, 128)) for a in range(m)
        ]
        small = [[spread[b][g + a : g + a + 1] for b in range(m)] for a in range(m)]
        inverse = small_inverse(small)
        picked = [[tile[g + a : g + a + 1] for a in range(m)] for tile in tiles]
        here = column[:1]
        for a in range(m):
            at = base + g + a
            for b in range(m):
                picked[home][b] = jnp.where(here == at, 1.0 if a == b else 0.0, picked[home][b])
            tiles[home] = jnp.where(column == at, 0.0, tiles[home])
        for t in range(len(tiles)):
            new = [sum(inverse[a][b] * picked[t][b] for b in range(m)) for a in range(m)]
            value = tiles[t]
            for a in range(m):
                value = value - spread[a] * new[a]
            for a in range(m):
                value = jnp.where(line == g + a, new[a], value)
            tiles[t] = value
    return jnp.concatenate(tiles, axis=1)


def posterior_kernel(gram_ref, ensemble_ref, out_ref, full, stack):
    n, b, m = 256, 64, 4
    packed_top = gram_ref[0]
    corner = gram_ref[1]
    line = lax.broadcasted_iota(jnp.int32, (128, 128), 0)
    column = lax.broadcasted_iota(jnp.int32, (128, 128), 1)
    shift = jnp.where(line == column, n - 1.0, 0.0)
    full[:128, :128] = packed_top[:, :128] + shift
    full[:128, 128:] = packed_top[:, 128:]
    full[128:, :128] = packed_top[:, 128:].T
    full[128:, 128:] = corner[:, :128] + shift
    proj = jnp.concatenate([corner[:1, 128:], corner[1:2, 128:]], axis=1)
    lanes = lax.broadcasted_iota(jnp.int32, (n, n), 1)
    stack[...] = jnp.zeros_like(stack)
    for k in range(0, n, b):
        solved = eliminate(full[k : k + b, :], k, m)
        home, base = k // 128 * 128, k % 128
        if base == 0:
            stack[...] = jnp.zeros_like(stack)
        elif k:
            stack[base - b : base] = jnp.zeros((b, n), F32)
        stack[base : base + b] = solved
        change = jnp.dot(full[:, home : home + 128], stack[...], precision=HIGH, preferred_element_type=F32)
        full[...] = jnp.where((lanes >= k) & (lanes < k + b), 0.0, full[...]) - change
        full[k : k + b] = solved
    inverse = full[...]
    mean_weights = jnp.sum(inverse * proj, axis=1, keepdims=True)
    rows = lax.broadcasted_iota(jnp.int32, (n, n), 0)
    weights = 0.5 * (n - 1.0) * inverse + jnp.where(rows == lanes, 0.5, 0.0) + mean_weights
    prior = ensemble_ref[...].astype(F32)
    prior_mean = jnp.mean(prior, axis=1, keepdims=True)
    moved = jnp.dot(prior - prior_mean, weights, precision=HIGH, preferred_element_type=F32)
    out_ref[...] = (prior_mean + moved).astype(BF16)


def per_device(ensemble, footprint, tile_index, tile_count, observed, obs_sigma):
    packed = summed_gram(ensemble, footprint, tile_index, tile_count, observed, obs_sigma)
    vmem = pl.BlockSpec(memory_space=pltpu.VMEM)
    return pl.pallas_call(
        posterior_kernel,
        out_shape=jax.ShapeDtypeStruct((256, 256), BF16),
        in_specs=[vmem, vmem],
        out_specs=vmem,
        scratch_shapes=[pltpu.VMEM((256, 256), F32), pltpu.VMEM((128, 256), F32)],
    )(packed.reshape(2, 128, 256), ensemble)


def solution(mesh):
    finer = Mesh(mesh.devices.reshape(4, 4, 16, 2), OBS_FLUX)
    placed = (
        P(OBS_FLUX, None),
        P(OBS, FLUX, None, None, None),
        P(OBS, FLUX, None),
        P(OBS, FLUX),
        P(OBS_FLUX),
        P(OBS_FLUX),
    )
    return jax.shard_map(
        per_device, mesh=finer, in_specs=placed, out_specs=P(OBS_FLUX, None), check_vma=False
    )
```

```python
import jax
import jax.numpy as jnp
from jax import lax
from jax.experimental import pallas as pl
from jax.experimental.pallas import tpu as pltpu
from jax.sharding import Mesh
from jax.sharding import PartitionSpec as P

OBS = ("obs_0", "obs_1")
FLUX = ("flux_0", "flux_1")
OBS_FLUX = OBS + FLUX
HIGH = lax.Precision.HIGHEST
MESH = pl.DeviceIdType.MESH
F32 = jnp.float32
BF16 = jnp.bfloat16
Z = 16
Q = 4


def update_kernel(
    index_ref, count_ref, ensemble_ref, footprint_ref, observed_ref, sigma_ref,
    gram_ref,
    region, prints, part, pair_out, pair_in,
    near_right_out, near_right_in, near_left_out, near_left_in, right_out, right_in, left_out, left_in,
    halves, half_in, pieces, pieces_in, z_out, z_in,
    local_sems, hop_send, hop_recv, pair_send, pair_recv, hop_z_send, hop_z_recv, half_sems,
    scatter_send, scatter_recv, z_send, z_recv, share_send, share_recv, give_send, give_recv, two_away,
):
    y, x = lax.axis_index("obs_0"), lax.axis_index("obs_1")
    z, c = lax.axis_index("flux_0"), lax.axis_index("flux_1")
    other = 1 - c

    def along_z(step):
        return (y, x, lax.rem(z + step + Z, Z), c)

    def in_plane(dy, dx):
        return (lax.rem(y + dy + Q, Q), lax.rem(x + dx + Q, Q), z, c)

    def hop(first, second):
        return in_plane(c * first + other * second, other * first + c * second)

    def owner(first, second):
        at = hop(first, second)
        return at[0] * Q + at[1]

    partner = (y, x, z, other)
    mine = y * Q + x

    load_prints = pltpu.make_async_copy(footprint_ref, prints, local_sems.at[0])
    load_prints.start()
    own = pltpu.make_async_copy(ensemble_ref, region.at[pl.ds(2 * mine, 2)], local_sems.at[1])
    own.start()

    ways = (hop(1, 0), hop(-1, 0)), (hop(0, 1), hop(0, -1))
    near_z = along_z(1), along_z(-1)
    barrier = pltpu.get_barrier_semaphore()
    for to in (partner, *ways[0], *ways[1], *near_z):
        pl.semaphore_signal(barrier, inc=1, device_id=to, device_id_type=MESH)
    pl.semaphore_wait(barrier, 7)
    for k in (0, 1):
        pl.semaphore_signal(two_away.at[k], inc=1, device_id=near_z[k], device_id_type=MESH)

    def piece(src, dst, sem, to):
        return pltpu.make_async_remote_copy(
            src_ref=src, dst_ref=dst, send_sem=hop_send.at[sem], recv_sem=hop_recv.at[sem],
            device_id=to, device_id_type=MESH,
        )

    sent = []

    def send(src, dst, sem, to):
        copy = piece(src, dst, sem, to)
        copy.start()
        sent.append(copy)

    def arrived(o, k, sem):
        piece(region.at[2 * o + k], region.at[2 * o + k], sem, partner).wait_recv()

    firsts = (0, -1, 1, 2)

    def start(src, o, k, axis, way, at):
        dst = region.at[2 * o + k]
        send(dst if src is None else src.at[k], dst, 6 * at + 2 * way + k, ways[axis][way])

    def relay(o, axis, way, at):
        dst = region.at[2 * o + way]
        send(dst, dst, 6 * at + 4 + way, ways[axis][way])

    def spread(o, k, n):
        start(None, o, k, 1, 0, 1 + n)
        start(None, o, k, 1, 1, 1 + n)

    def pass_on(n):
        for way in (0, 1):
            o = owner(firsts[n], 2 * way - 1)
            arrived(o, way, 6 + 6 * n + 3 * way)
            relay(o, 1, way, 1 + n)

    for turn in (0, 1):
        for axis in (0, 1):
            for way in (0, 1):
                start(ensemble_ref, mine, way if turn == 0 else 1 - way, axis, way, axis)
    behind, ahead, across = owner(-1, 0), owner(1, 0), owner(2, 0)
    arrived(behind, 0, 0)
    relay(behind, 0, 0, 0)
    spread(behind, 0, 1)
    arrived(ahead, 1, 3)
    relay(ahead, 0, 1, 0)
    spread(ahead, 1, 2)
    pass_on(0)
    arrived(behind, 1, 1)
    spread(behind, 1, 1)
    arrived(ahead, 0, 2)
    spread(ahead, 0, 2)
    arrived(across, 0, 4)
    spread(across, 0, 3)
    arrived(across, 1, 5)
    spread(across, 1, 3)
    pass_on(1)
    pass_on(2)
    pass_on(3)
    for n in range(4):
        lower, upper, far = (owner(firsts[n], k) for k in (-1, 1, 2))
        arrived(lower, 1, 6 + 6 * n + 1)
        arrived(upper, 0, 6 + 6 * n + 2)
        arrived(far, 0, 6 + 6 * n + 4)
        arrived(far, 1, 6 + 6 * n + 5)
    own.wait()
    load_prints.wait()

    def pair_copy(t):
        return pltpu.make_async_remote_copy(
            src_ref=pair_out.at[t], dst_ref=pair_in.at[t], send_sem=pair_send.at[t],
            recv_sem=pair_recv.at[t], device_id=partner, device_id_type=MESH,
        )

    def offset(t):
        half = t // 2
        return jnp.where(lax.rem(t, 2) == 0, 8 - half, 9 + half)

    def block(t):
        b = lax.rem(z + offset(t), Z)
        count = count_ref[b]
        lhs, rhs = [], []
        for s in range(8):
            values = prints[b, s]
            lhs.append(jnp.where(s < count, values, jnp.zeros_like(values)))
            rhs.append(region[index_ref[s, b]])
        total = jnp.dot(
            jnp.concatenate(lhs, axis=1), jnp.concatenate(rhs, axis=0), preferred_element_type=F32
        )
        part[t] = jnp.where(c == 0, total[:64], total[64:])
        pair_out[t] = jnp.where(c == 0, total[64:], total[:64]).astype(BF16)
        pair_copy(t).start()

    def z_hop(src, dst, k, i, step):
        return pltpu.make_async_remote_copy(
            src_ref=src.at[i], dst_ref=dst.at[i], send_sem=hop_z_send.at[k, i],
            recv_sem=hop_z_recv.at[k, i], device_id=along_z(step), device_id_type=MESH,
        )

    def near_right(i):
        return z_hop(near_right_out, near_right_in, 0, i, 1)

    def near_left(i):
        return z_hop(near_left_out, near_left_in, 1, i, -1)

    def right_copy(i):
        return z_hop(right_out, right_in, 2, i, 2 - i // 3)

    def left_copy(i):
        return z_hop(left_out, left_in, 3, i, i // 3 - 2)

    def own_sum(t):
        pair_copy(t).wait_recv()
        return part[t] + pair_in[t].astype(F32)

    def blocks(start, stop):
        @pl.loop(start, stop)
        def _(t):
            block(t)

    def near_sends(t):
        near_left_out[t // 4] = own_sum(t).astype(BF16)
        near_left(t // 4).start()
        near_right_out[t // 4 + 1] = own_sum(t + 1).astype(BF16)
        near_right(t // 4 + 1).start()

    def left_step(i):
        total = own_sum(4 * i + 1)
        if i:
            near_left(i - 1).wait_recv()
            left_copy(i - 1).wait_recv()
            total = total + near_left_in[i - 1].astype(F32) + left_in[i - 1].astype(F32)
        left_out[i] = total.astype(BF16)
        left_copy(i).start()

    def right_step(i):
        total = own_sum(4 * i + 2)
        near_right(i).wait_recv()
        total = total + near_right_in[i].astype(F32)
        if i:
            right_copy(i - 1).wait_recv()
            total = total + right_in[i - 1].astype(F32)
        right_out[i] = total.astype(BF16)
        right_copy(i).start()

    blocks(0, 3)
    for k in (0, 1):
        pl.semaphore_wait(two_away.at[k], 1)
    near_right_out[0] = own_sum(0).astype(BF16)
    near_right(0).start()
    left_step(0)
    blocks(3, 7)
    near_sends(3)
    right_step(0)
    blocks(7, 11)
    near_sends(7)
    left_step(1)
    blocks(11, 16)
    near_sends(11)
    right_step(1)
    left_step(2)
    right_step(2)
    left_step(3)
    right_step(3)

    evolved = own_sum(15)
    left_copy(3).wait_recv()
    evolved = evolved + left_in[3].astype(F32)
    right_copy(3).wait_recv()
    evolved = evolved + right_in[3].astype(F32)

    lines = lax.broadcasted_iota(jnp.int32, (64, 64), 0)
    columns = lax.broadcasted_iota(jnp.int32, (64, 64), 1)

    def upright(row):
        return jnp.sum(jnp.where(lines == columns, row, 0.0), axis=1, keepdims=True)

    sigma = upright(sigma_ref[...])
    mean_sim = jnp.mean(evolved, axis=1, keepdims=True)
    scaled = (evolved - mean_sim) / sigma
    innovation = (upright(observed_ref[...]) - mean_sim) / sigma
    gram = lax.dot_general(
        scaled, scaled, (((0,), (0,)), ((), ())), precision=HIGH,
        preferred_element_type=F32,
    )
    proj = jnp.sum(innovation * scaled, axis=0, keepdims=True)
    halves[0] = gram[:128]
    halves[1, :, :128] = gram[128:, 128:]
    line = lax.broadcasted_iota(jnp.int32, (128, 128), 0)
    halves[1, :, 128:] = jnp.where(
        line == 0, proj[:, :128], jnp.where(line == 1, proj[:, 128:], 0.0)
    )

    half_copy = pltpu.make_async_remote_copy(
        src_ref=halves.at[other], dst_ref=half_in, send_sem=half_sems.at[0],
        recv_sem=half_sems.at[1], device_id=partner, device_id_type=MESH,
    )
    half_copy.start()
    half_copy.wait_recv()
    pieces[...] = (halves[c] + half_in[...]).reshape(16, 8, 256)
    plane = ((2, 2), (1, 2), (3, 2), (2, 1), (2, 3), (0, 2), (2, 0), (1, 1), (1, 3), (3, 1), (3, 3),
             (0, 1), (0, 3), (1, 0), (3, 0))

    def spot(dy, dx):
        at = in_plane(dy, dx)
        return at[0] * Q + at[1]

    def scatter_copy(t):
        return pltpu.make_async_remote_copy(
            src_ref=pieces.at[spot(*plane[t])], dst_ref=pieces_in.at[t], send_sem=scatter_send.at[t],
            recv_sem=scatter_recv.at[t], device_id=in_plane(*plane[t]), device_id_type=MESH,
        )

    for t in range(15):
        scatter_copy(t).start()
    summed = pieces[mine]
    for t in reversed(range(15)):
        scatter_copy(t).wait_recv()
        summed = summed + pieces_in[t]
    z_out[...] = summed

    def z_copy(t):
        return pltpu.make_async_remote_copy(
            src_ref=z_out, dst_ref=z_in.at[t], send_sem=z_send.at[t],
            recv_sem=z_recv.at[t], device_id=along_z(offset(t)), device_id_type=MESH,
        )

    @pl.loop(0, Z - 1)
    def _(t):
        z_copy(t).start()

    def add_z(i, total):
        t = Z - 2 - i
        z_copy(t).wait_recv()
        return total + z_in[t]

    gram_ref[c, mine] = lax.fori_loop(0, Z - 1, add_z, summed)

    def share_copy(t, at):
        return pltpu.make_async_remote_copy(
            src_ref=gram_ref.at[c, at], dst_ref=gram_ref.at[c, at], send_sem=share_send.at[t],
            recv_sem=share_recv.at[t], device_id=in_plane(*plane[t]), device_id_type=MESH,
        )

    def give_copy(t, half, at):
        return pltpu.make_async_remote_copy(
            src_ref=gram_ref.at[half, at], dst_ref=gram_ref.at[half, at], send_sem=give_send.at[t],
            recv_sem=give_recv.at[t], device_id=partner, device_id_type=MESH,
        )

    def origin(t):
        dy, dx = plane[t]
        return spot(-dy, -dx)

    for t in range(15):
        share_copy(t, mine).start()
    give_copy(15, c, mine).start()
    for t in reversed(range(15)):
        share_copy(t, origin(t)).wait_recv()
        give_copy(t, c, origin(t)).start()
    give_copy(15, other, mine).wait_recv()
    for t in reversed(range(15)):
        give_copy(t, other, origin(t)).wait_recv()

    for copy in sent:
        copy.wait_send()
    half_copy.wait_send()

    @pl.loop(0, 16)
    def _(t):
        pair_copy(t).wait_send()
        give_copy(t, c, mine).wait_send()

    @pl.loop(0, 4)
    def _(i):
        near_right(i).wait_send()
        right_copy(i).wait_send()
        left_copy(i).wait_send()

    @pl.loop(0, 3)
    def _(i):
        near_left(i).wait_send()

    @pl.loop(0, Z - 1)
    def _(t):
        z_copy(t).wait_send()

    for t in range(15):
        scatter_copy(t).wait_send()
        share_copy(t, mine).wait_send()


def summed_gram(ensemble, footprint, tile_index, tile_count, observed, obs_sigma):
    dma = pltpu.SemaphoreType.DMA
    vmem = pltpu.VMEM
    return pl.pallas_call(
        update_kernel,
        out_shape=jax.ShapeDtypeStruct((2, Z, 8, 256), F32),
        in_specs=[
            pl.BlockSpec(memory_space=pltpu.SMEM),
            pl.BlockSpec(memory_space=pltpu.SMEM),
            pl.BlockSpec(memory_space=pl.ANY),
            pl.BlockSpec(memory_space=pl.ANY),
            pl.BlockSpec(memory_space=vmem),
            pl.BlockSpec(memory_space=vmem),
        ],
        out_specs=pl.BlockSpec(memory_space=vmem),
        scratch_shapes=[
            vmem((32, 128, 256), BF16),
            vmem((16, 8, 128, 128), BF16),
            vmem((16, 64, 256), F32),
            vmem((16, 64, 256), BF16),
            vmem((16, 64, 256), BF16),
            *[vmem((4, 64, 256), BF16)] * 8,
            vmem((2, 128, 256), F32),
            vmem((128, 256), F32),
            vmem((16, 8, 256), F32),
            vmem((15, 8, 256), F32),
            vmem((8, 256), F32),
            vmem((15, 8, 256), F32),
            dma((2,)),
            dma((30,)),
            dma((30,)),
            dma((16,)),
            dma((16,)),
            dma((4, 4)),
            dma((4, 4)),
            dma((2,)),
            *[dma((15,))] * 6,
            dma((16,)),
            dma((16,)),
            pltpu.SemaphoreType.REGULAR((2,)),
        ],
        compiler_params=pltpu.CompilerParams(collective_id=0, has_side_effects=True),
    )(
        tile_index.reshape(16, 8).T, tile_count.reshape(16), ensemble.reshape(2, 128, 256),
        footprint.reshape(16, 8, 128, 128), observed.reshape(1, 64), obs_sigma.reshape(1, 64),
    )


def small_inverse(s):
    n = len(s)
    if n == 1:
        return [[1.0 / s[0][0]]]
    if n == 2:
        scale = 1.0 / (s[0][0] * s[1][1] - s[0][1] * s[0][1])
        off = -s[0][1] * scale
        return [[s[1][1] * scale, off], [off, s[0][0] * scale]]
    h = n // 2
    low, high = range(h), range(h, n)
    e = small_inverse([[s[i][j] for j in low] for i in low])
    ef = [[sum(e[i][k] * s[k][j] for k in low) for j in high] for i in low]
    rest = [[s[i][j] - sum(s[k][i] * ef[k][j - h] for k in low) for j in high] for i in high]
    r = small_inverse(rest)
    off = [[-sum(ef[i][k] * r[k][j] for k in range(n - h)) for j in range(n - h)] for i in low]
    top = [[e[i][j] - sum(off[i][k] * ef[j][k] for k in range(n - h)) for j in low] for i in low]
    out = [[None] * n for _ in range(n)]
    for i in range(n):
        for j in range(n):
            a, b = min(i, j), max(i, j)
            out[i][j] = top[a][b] if b < h else (off[a][b - h] if a < h else r[a - h][b - h])
    return out


def eliminate(panel, first, m):
    rows, lanes = panel.shape
    line = lax.broadcasted_iota(jnp.int32, (rows, 128), 0)
    column = lax.broadcasted_iota(jnp.int32, (rows, 128), 1)
    tiles = [panel[:, 128 * t : 128 * t + 128] for t in range(lanes // 128)]
    home, base = first // 128, first % 128
    here = column[:1]
    span = range(m)

    def lifted(top, bottom, lane):
        return jnp.broadcast_to(tiles[home][top:bottom, lane : lane + 1], (bottom - top, 128))

    small = None
    for g in range(0, rows, m):
        at = base + g
        spread = [lifted(0, rows, at + a) for a in span]
        if small is None:
            small = [[spread[b][g + a : g + a + 1] for b in span] for a in span]
        inverse = small_inverse(small)
        if g + m < rows:
            ahead = [lifted(g, g + 2 * m, at + m + j) for j in span]
            side = [[ahead[j][b : b + 1] for b in span] for j in span]
            row = [[sum(inverse[a][b] * side[j][b] for b in span) for j in span] for a in span]
            small = [[None] * m for _ in span]
            for i in span:
                for j in range(i, m):
                    small[i][j] = ahead[j][m + i : m + i + 1] - sum(side[i][a] * row[a][j] for a in span)
                    small[j][i] = small[i][j]
        else:
            small = None
        picked = [[tile[g + a : g + a + 1] for a in span] for tile in tiles]
        for a in span:
            for b in span:
                picked[home][b] = jnp.where(here == at + a, 1.0 if a == b else 0.0, picked[home][b])
        tiles[home] = jnp.where((column >= at) & (column < at + m), 0.0, tiles[home])
        for t in range(len(tiles)):
            new = [sum(inverse[a][b] * picked[t][b] for b in span) for a in span]
            value = tiles[t]
            for a in span:
                value = value - spread[a] * new[a]
            for a in span:
                value = jnp.where(line == g + a, new[a], value)
            tiles[t] = value
    return jnp.concatenate(tiles, axis=1)


def posterior_kernel(gram_ref, ensemble_ref, out_ref, full):
    n, b, m = 256, 64, 4
    packed_top = gram_ref[0]
    corner = gram_ref[1]
    line = lax.broadcasted_iota(jnp.int32, (128, 128), 0)
    column = lax.broadcasted_iota(jnp.int32, (128, 128), 1)
    shift = jnp.where(line == column, n - 1.0, 0.0)
    full[:128, :128] = packed_top[:, :128] + shift
    full[:128, 128:] = packed_top[:, 128:]
    full[128:, :128] = packed_top[:, 128:].T
    full[128:, 128:] = corner[:, :128] + shift
    proj = jnp.concatenate([corner[:1, 128:], corner[1:2, 128:]], axis=1)
    lanes = lax.broadcasted_iota(jnp.int32, (n, n), 1)
    panels = [full[k : k + b] for k in range(0, n, b)]
    lane = lanes[:b]
    for p in range(n // b):
        k = p * b
        solved = eliminate(panels[p], k, m)
        home, base = k // 128 * 128, k % 128
        parts = [jnp.zeros((base, n), F32), solved, jnp.zeros((128 - b - base, n), F32)]
        wide = jnp.concatenate([q for q in parts if q.shape[0]], axis=0)
        inside = (lane >= k) & (lane < k + b)
        for step in range(1, n // b):
            i = (p + step) % (n // b)
            change = jnp.dot(panels[i][:, home : home + 128], wide, precision=HIGH, preferred_element_type=F32)
            panels[i] = jnp.where(inside, 0.0, panels[i]) - change
        panels[p] = solved
    inverse = jnp.concatenate(panels, axis=0)
    mean_weights = jnp.sum(inverse * proj, axis=1, keepdims=True)
    rows = lax.broadcasted_iota(jnp.int32, (n, n), 0)
    weights = 0.5 * (n - 1.0) * inverse + jnp.where(rows == lanes, 0.5, 0.0) + mean_weights
    prior = ensemble_ref[...].astype(F32)
    prior_mean = jnp.mean(prior, axis=1, keepdims=True)
    moved = jnp.dot(prior - prior_mean, weights, precision=HIGH, preferred_element_type=F32)
    out_ref[...] = (prior_mean + moved).astype(BF16)


def per_device(ensemble, footprint, tile_index, tile_count, observed, obs_sigma):
    packed = summed_gram(ensemble, footprint, tile_index, tile_count, observed, obs_sigma)
    vmem = pl.BlockSpec(memory_space=pltpu.VMEM)
    return pl.pallas_call(
        posterior_kernel,
        out_shape=jax.ShapeDtypeStruct((256, 256), BF16),
        in_specs=[vmem, vmem],
        out_specs=vmem,
        scratch_shapes=[pltpu.VMEM((256, 256), F32)],
    )(packed.reshape(2, 128, 256), ensemble)


def solution(mesh):
    finer = Mesh(mesh.devices.reshape(4, 4, 16, 2), OBS_FLUX)
    placed = (
        P(OBS_FLUX, None),
        P(OBS, FLUX, None, None, None),
        P(OBS, FLUX, None),
        P(OBS, FLUX),
        P(OBS_FLUX),
        P(OBS_FLUX),
    )
    return jax.shard_map(
        per_device, mesh=finer, in_specs=placed, out_specs=P(OBS_FLUX, None), check_vma=False
    )
```

```python
import jax
import jax.numpy as jnp
from jax import lax
from jax.experimental import pallas as pl
from jax.experimental.pallas import tpu as pltpu
from jax.sharding import Mesh
from jax.sharding import PartitionSpec as P

OBS = ("obs_0", "obs_1")
FLUX = ("flux_0", "flux_1")
OBS_FLUX = OBS + FLUX
HIGH = lax.Precision.HIGHEST
MESH = pl.DeviceIdType.MESH
F32 = jnp.float32
BF16 = jnp.bfloat16
Z = 16
Q = 4


def update_kernel(
    index_ref, count_ref, ensemble_ref, footprint_ref, observed_ref, sigma_ref,
    gram_ref,
    region, prints, part, pair_out, pair_in,
    near_right_out, near_right_in, near_left_out, near_left_in, right_out, right_in, left_out, left_in,
    halves, half_in, pieces, pieces_in, z_out, z_in,
    local_sems, hop_send, hop_recv, pair_send, pair_recv, hop_z_send, hop_z_recv, half_sems,
    scatter_send, scatter_recv, z_send, z_recv, share_send, share_recv, give_send, give_recv, two_away,
):
    y, x = lax.axis_index("obs_0"), lax.axis_index("obs_1")
    z, c = lax.axis_index("flux_0"), lax.axis_index("flux_1")
    other = 1 - c

    def along_z(step):
        return (y, x, lax.rem(z + step + Z, Z), c)

    def in_plane(dy, dx):
        return (lax.rem(y + dy + Q, Q), lax.rem(x + dx + Q, Q), z, c)

    def hop(first, second):
        return in_plane(c * first + other * second, other * first + c * second)

    def owner(first, second):
        at = hop(first, second)
        return at[0] * Q + at[1]

    partner = (y, x, z, other)
    mine = y * Q + x

    load_prints = pltpu.make_async_copy(footprint_ref, prints, local_sems.at[0])
    own = pltpu.make_async_copy(ensemble_ref, region.at[pl.ds(2 * mine, 2)], local_sems.at[1])
    own.start()

    ways = (hop(1, 0), hop(-1, 0)), (hop(0, 1), hop(0, -1))
    near_z = along_z(1), along_z(-1)
    barrier = pltpu.get_barrier_semaphore()
    for to in (partner, *ways[0], *ways[1], *near_z):
        pl.semaphore_signal(barrier, inc=1, device_id=to, device_id_type=MESH)
    pl.semaphore_wait(barrier, 7)
    for k in (0, 1):
        pl.semaphore_signal(two_away.at[k], inc=1, device_id=near_z[k], device_id_type=MESH)

    def piece(src, dst, sem, to):
        return pltpu.make_async_remote_copy(
            src_ref=src, dst_ref=dst, send_sem=hop_send.at[sem], recv_sem=hop_recv.at[sem],
            device_id=to, device_id_type=MESH,
        )

    sent = []

    def send(src, dst, sem, to):
        copy = piece(src, dst, sem, to)
        copy.start()
        sent.append(copy)

    def arrived(o, k, sem):
        piece(region.at[2 * o + k], region.at[2 * o + k], sem, partner).wait_recv()

    firsts = (0, -1, 1, 2)

    def start(o, k, axis, way, at):
        dst = region.at[2 * o + k]
        send(dst, dst, 6 * at + 2 * way + k, ways[axis][way])

    def relay(o, axis, way, at):
        dst = region.at[2 * o + way]
        send(dst, dst, 6 * at + 4 + way, ways[axis][way])

    def spread(o, k, n):
        start(o, k, 1, 0, 1 + n)
        start(o, k, 1, 1, 1 + n)

    def pass_on(n):
        for way in (0, 1):
            o = owner(firsts[n], 2 * way - 1)
            arrived(o, way, 6 + 6 * n + 3 * way)
            relay(o, 1, way, 1 + n)

    own.wait()
    for turn in (0, 1):
        for axis in (0, 1):
            for way in (0, 1):
                start(mine, way if turn == 0 else 1 - way, axis, way, axis)
    load_prints.start()
    behind, ahead, across = owner(-1, 0), owner(1, 0), owner(2, 0)
    arrived(behind, 0, 0)
    relay(behind, 0, 0, 0)
    spread(behind, 0, 1)
    arrived(ahead, 1, 3)
    relay(ahead, 0, 1, 0)
    spread(ahead, 1, 2)
    pass_on(0)
    arrived(behind, 1, 1)
    spread(behind, 1, 1)
    arrived(ahead, 0, 2)
    spread(ahead, 0, 2)
    arrived(across, 0, 4)
    spread(across, 0, 3)
    arrived(across, 1, 5)
    spread(across, 1, 3)
    pass_on(1)
    pass_on(2)
    pass_on(3)
    for n in range(4):
        lower, upper, far = (owner(firsts[n], k) for k in (-1, 1, 2))
        arrived(lower, 1, 6 + 6 * n + 1)
        arrived(upper, 0, 6 + 6 * n + 2)
        arrived(far, 0, 6 + 6 * n + 4)
        arrived(far, 1, 6 + 6 * n + 5)
    load_prints.wait()

    def pair_copy(t):
        return pltpu.make_async_remote_copy(
            src_ref=pair_out.at[t], dst_ref=pair_in.at[t], send_sem=pair_send.at[t],
            recv_sem=pair_recv.at[t], device_id=partner, device_id_type=MESH,
        )

    def offset(t):
        half = t // 2
        return jnp.where(lax.rem(t, 2) == 0, 8 - half, 9 + half)

    def block(t):
        b = lax.rem(z + offset(t), Z)
        count = count_ref[b]
        lhs, rhs = [], []
        for s in range(8):
            values = prints[b, s]
            lhs.append(jnp.where(s < count, values, jnp.zeros_like(values)))
            rhs.append(region[index_ref[s, b]])
        total = jnp.dot(
            jnp.concatenate(lhs, axis=1), jnp.concatenate(rhs, axis=0), preferred_element_type=F32
        )
        part[t] = jnp.where(c == 0, total[:64], total[64:])
        pair_out[t] = jnp.where(c == 0, total[64:], total[:64]).astype(BF16)
        pair_copy(t).start()

    def z_hop(src, dst, k, i, step):
        return pltpu.make_async_remote_copy(
            src_ref=src.at[i], dst_ref=dst.at[i], send_sem=hop_z_send.at[k, i],
            recv_sem=hop_z_recv.at[k, i], device_id=along_z(step), device_id_type=MESH,
        )

    def near_right(i):
        return z_hop(near_right_out, near_right_in, 0, i, 1)

    def near_left(i):
        return z_hop(near_left_out, near_left_in, 1, i, -1)

    def right_copy(i):
        return z_hop(right_out, right_in, 2, i, 2 - i // 3)

    def left_copy(i):
        return z_hop(left_out, left_in, 3, i, i // 3 - 2)

    def own_sum(t):
        pair_copy(t).wait_recv()
        return part[t] + pair_in[t].astype(F32)

    def blocks(start, stop):
        @pl.loop(start, stop)
        def _(t):
            block(t)

    def near_sends(t):
        near_left_out[t // 4] = own_sum(t).astype(BF16)
        near_left(t // 4).start()
        near_right_out[t // 4 + 1] = own_sum(t + 1).astype(BF16)
        near_right(t // 4 + 1).start()

    def left_step(i):
        total = own_sum(4 * i + 1)
        if i:
            near_left(i - 1).wait_recv()
            left_copy(i - 1).wait_recv()
            total = total + near_left_in[i - 1].astype(F32) + left_in[i - 1].astype(F32)
        left_out[i] = total.astype(BF16)
        left_copy(i).start()

    def right_step(i):
        total = own_sum(4 * i + 2)
        near_right(i).wait_recv()
        total = total + near_right_in[i].astype(F32)
        if i:
            right_copy(i - 1).wait_recv()
            total = total + right_in[i - 1].astype(F32)
        right_out[i] = total.astype(BF16)
        right_copy(i).start()

    blocks(0, 3)
    for k in (0, 1):
        pl.semaphore_wait(two_away.at[k], 1)
    near_right_out[0] = own_sum(0).astype(BF16)
    near_right(0).start()
    left_step(0)
    blocks(3, 7)
    near_sends(3)
    right_step(0)
    blocks(7, 11)
    near_sends(7)
    left_step(1)
    blocks(11, 16)
    near_sends(11)
    for copy in sent:
        copy.wait_send()
    right_step(1)
    left_step(2)
    right_step(2)
    left_step(3)
    right_step(3)

    evolved = own_sum(15)
    left_copy(3).wait_recv()
    evolved = evolved + left_in[3].astype(F32)
    right_copy(3).wait_recv()
    evolved = evolved + right_in[3].astype(F32)

    lines = lax.broadcasted_iota(jnp.int32, (64, 64), 0)
    columns = lax.broadcasted_iota(jnp.int32, (64, 64), 1)

    def upright(row):
        return jnp.sum(jnp.where(lines == columns, row, 0.0), axis=1, keepdims=True)

    sigma = upright(sigma_ref[...])
    mean_sim = jnp.mean(evolved, axis=1, keepdims=True)
    scaled = (evolved - mean_sim) / sigma
    innovation = (upright(observed_ref[...]) - mean_sim) / sigma
    gram = lax.dot_general(
        scaled, scaled, (((0,), (0,)), ((), ())), precision=HIGH,
        preferred_element_type=F32,
    )
    proj = jnp.sum(innovation * scaled, axis=0, keepdims=True)
    halves[0] = gram[:128]
    halves[1, :, :128] = gram[128:, 128:]
    line = lax.broadcasted_iota(jnp.int32, (128, 128), 0)
    halves[1, :, 128:] = jnp.where(
        line == 0, proj[:, :128], jnp.where(line == 1, proj[:, 128:], 0.0)
    )

    half_copy = pltpu.make_async_remote_copy(
        src_ref=halves.at[other], dst_ref=half_in, send_sem=half_sems.at[0],
        recv_sem=half_sems.at[1], device_id=partner, device_id_type=MESH,
    )
    half_copy.start()
    half_copy.wait_recv()
    pieces[...] = (halves[c] + half_in[...]).reshape(16, 8, 256)
    plane = ((2, 2), (1, 2), (3, 2), (2, 1), (2, 3), (0, 2), (2, 0), (1, 1), (1, 3), (3, 1), (3, 3),
             (0, 1), (0, 3), (1, 0), (3, 0))

    def spot(dy, dx):
        at = in_plane(dy, dx)
        return at[0] * Q + at[1]

    def scatter_copy(t):
        return pltpu.make_async_remote_copy(
            src_ref=pieces.at[spot(*plane[t])], dst_ref=pieces_in.at[t], send_sem=scatter_send.at[t],
            recv_sem=scatter_recv.at[t], device_id=in_plane(*plane[t]), device_id_type=MESH,
        )

    for t in range(15):
        scatter_copy(t).start()
    summed = pieces[mine]
    for t in reversed(range(15)):
        scatter_copy(t).wait_recv()
        summed = summed + pieces_in[t]
    z_out[...] = summed

    def z_copy(t):
        return pltpu.make_async_remote_copy(
            src_ref=z_out, dst_ref=z_in.at[t], send_sem=z_send.at[t],
            recv_sem=z_recv.at[t], device_id=along_z(offset(t)), device_id_type=MESH,
        )

    @pl.loop(0, Z - 1)
    def _(t):
        z_copy(t).start()

    half_copy.wait_send()

    @pl.loop(0, 16)
    def _(t):
        pair_copy(t).wait_send()

    @pl.loop(0, 4)
    def _(i):
        near_right(i).wait_send()
        right_copy(i).wait_send()
        left_copy(i).wait_send()

    @pl.loop(0, 3)
    def _(i):
        near_left(i).wait_send()

    for t in range(15):
        scatter_copy(t).wait_send()

    def add_z(i, total):
        t = Z - 2 - i
        z_copy(t).wait_recv()
        return total + z_in[t]

    gram_ref[c, mine] = lax.fori_loop(0, Z - 1, add_z, summed)

    def share_copy(t, at):
        return pltpu.make_async_remote_copy(
            src_ref=gram_ref.at[c, at], dst_ref=gram_ref.at[c, at], send_sem=share_send.at[t],
            recv_sem=share_recv.at[t], device_id=in_plane(*plane[t]), device_id_type=MESH,
        )

    def give_copy(t, half, at):
        return pltpu.make_async_remote_copy(
            src_ref=gram_ref.at[half, at], dst_ref=gram_ref.at[half, at], send_sem=give_send.at[t],
            recv_sem=give_recv.at[t], device_id=partner, device_id_type=MESH,
        )

    def origin(t):
        dy, dx = plane[t]
        return spot(-dy, -dx)

    for t in range(15):
        share_copy(t, mine).start()
    give_copy(15, c, mine).start()

    @pl.loop(0, Z - 1)
    def _(t):
        z_copy(t).wait_send()

    for t in reversed(range(15)):
        share_copy(t, origin(t)).wait_recv()
        give_copy(t, c, origin(t)).start()
    give_copy(15, other, mine).wait_recv()
    for t in reversed(range(15)):
        give_copy(t, other, origin(t)).wait_recv()

    @pl.loop(0, 16)
    def _(t):
        give_copy(t, c, mine).wait_send()

    for t in range(15):
        share_copy(t, mine).wait_send()


def summed_gram(ensemble, footprint, tile_index, tile_count, observed, obs_sigma):
    dma = pltpu.SemaphoreType.DMA
    vmem = pltpu.VMEM
    return pl.pallas_call(
        update_kernel,
        out_shape=jax.ShapeDtypeStruct((2, Z, 8, 256), F32),
        in_specs=[
            pl.BlockSpec(memory_space=pltpu.SMEM),
            pl.BlockSpec(memory_space=pltpu.SMEM),
            pl.BlockSpec(memory_space=pl.ANY),
            pl.BlockSpec(memory_space=pl.ANY),
            pl.BlockSpec(memory_space=vmem),
            pl.BlockSpec(memory_space=vmem),
        ],
        out_specs=pl.BlockSpec(memory_space=vmem),
        scratch_shapes=[
            vmem((32, 128, 256), BF16),
            vmem((16, 8, 128, 128), BF16),
            vmem((16, 64, 256), F32),
            vmem((16, 64, 256), BF16),
            vmem((16, 64, 256), BF16),
            *[vmem((4, 64, 256), BF16)] * 8,
            vmem((2, 128, 256), F32),
            vmem((128, 256), F32),
            vmem((16, 8, 256), F32),
            vmem((15, 8, 256), F32),
            vmem((8, 256), F32),
            vmem((15, 8, 256), F32),
            dma((2,)),
            dma((30,)),
            dma((30,)),
            dma((16,)),
            dma((16,)),
            dma((4, 4)),
            dma((4, 4)),
            dma((2,)),
            *[dma((15,))] * 6,
            dma((16,)),
            dma((16,)),
            pltpu.SemaphoreType.REGULAR((2,)),
        ],
        compiler_params=pltpu.CompilerParams(collective_id=0, has_side_effects=True),
    )(
        tile_index.reshape(16, 8).T, tile_count.reshape(16), ensemble.reshape(2, 128, 256),
        footprint.reshape(16, 8, 128, 128), observed.reshape(1, 64), obs_sigma.reshape(1, 64),
    )


def small_inverse(s):
    n = len(s)
    if n == 1:
        return [[1.0 / s[0][0]]]
    if n == 2:
        scale = 1.0 / (s[0][0] * s[1][1] - s[0][1] * s[0][1])
        off = -s[0][1] * scale
        return [[s[1][1] * scale, off], [off, s[0][0] * scale]]
    h = n // 2
    low, high = range(h), range(h, n)
    e = small_inverse([[s[i][j] for j in low] for i in low])
    ef = [[sum(e[i][k] * s[k][j] for k in low) for j in high] for i in low]
    rest = [[s[i][j] - sum(s[k][i] * ef[k][j - h] for k in low) for j in high] for i in high]
    r = small_inverse(rest)
    off = [[-sum(ef[i][k] * r[k][j] for k in range(n - h)) for j in range(n - h)] for i in low]
    top = [[e[i][j] - sum(off[i][k] * ef[j][k] for k in range(n - h)) for j in low] for i in low]
    out = [[None] * n for _ in range(n)]
    for i in range(n):
        for j in range(n):
            a, b = min(i, j), max(i, j)
            out[i][j] = top[a][b] if b < h else (off[a][b - h] if a < h else r[a - h][b - h])
    return out


def eliminate(panel, first, m):
    rows, lanes = panel.shape
    line = lax.broadcasted_iota(jnp.int32, (rows, 128), 0)
    column = lax.broadcasted_iota(jnp.int32, (rows, 128), 1)
    tiles = [panel[:, 128 * t : 128 * t + 128] for t in range(lanes // 128)]
    home, base = first // 128, first % 128
    here = column[:1]
    span = range(m)

    def lifted(top, bottom, lane):
        return jnp.broadcast_to(tiles[home][top:bottom, lane : lane + 1], (bottom - top, 128))

    small = None
    for g in range(0, rows, m):
        at = base + g
        spread = [lifted(0, rows, at + a) for a in span]
        if small is None:
            small = [[spread[b][g + a : g + a + 1] for b in span] for a in span]
        inverse = small_inverse(small)
        if g + m < rows:
            ahead = [lifted(g, g + 2 * m, at + m + j) for j in span]
            side = [[ahead[j][b : b + 1] for b in span] for j in span]
            row = [[sum(inverse[a][b] * side[j][b] for b in span) for j in span] for a in span]
            small = [[None] * m for _ in span]
            for i in span:
                for j in range(i, m):
                    small[i][j] = ahead[j][m + i : m + i + 1] - sum(side[i][a] * row[a][j] for a in span)
                    small[j][i] = small[i][j]
        else:
            small = None
        picked = [[tile[g + a : g + a + 1] for a in span] for tile in tiles]
        for a in span:
            for b in span:
                picked[home][b] = jnp.where(here == at + a, 1.0 if a == b else 0.0, picked[home][b])
        tiles[home] = jnp.where((column >= at) & (column < at + m), 0.0, tiles[home])
        for t in range(len(tiles)):
            new = [sum(inverse[a][b] * picked[t][b] for b in span) for a in span]
            value = tiles[t]
            for a in span:
                value = value - spread[a] * new[a]
            for a in span:
                value = jnp.where(line == g + a, new[a], value)
            tiles[t] = value
    return jnp.concatenate(tiles, axis=1)


def posterior_kernel(gram_ref, ensemble_ref, out_ref, full):
    n, b, m = 256, 64, 4
    packed_top = gram_ref[0]
    corner = gram_ref[1]
    line = lax.broadcasted_iota(jnp.int32, (128, 128), 0)
    column = lax.broadcasted_iota(jnp.int32, (128, 128), 1)
    shift = jnp.where(line == column, n - 1.0, 0.0)
    full[:128, :128] = packed_top[:, :128] + shift
    full[:128, 128:] = packed_top[:, 128:]
    full[128:, :128] = packed_top[:, 128:].T
    full[128:, 128:] = corner[:, :128] + shift
    proj = jnp.concatenate([corner[:1, 128:], corner[1:2, 128:]], axis=1)
    lanes = lax.broadcasted_iota(jnp.int32, (n, n), 1)
    panels = [full[k : k + b] for k in range(0, n, b)]
    lane = lanes[:b]
    for p in range(n // b):
        k = p * b
        solved = eliminate(panels[p], k, m)
        home, base = k // 128 * 128, k % 128
        parts = [jnp.zeros((base, n), F32), solved, jnp.zeros((128 - b - base, n), F32)]
        wide = jnp.concatenate([q for q in parts if q.shape[0]], axis=0)
        inside = (lane >= k) & (lane < k + b)
        for step in range(1, n // b):
            i = (p + step) % (n // b)
            change = jnp.dot(panels[i][:, home : home + 128], wide, precision=HIGH, preferred_element_type=F32)
            panels[i] = jnp.where(inside, 0.0, panels[i]) - change
        panels[p] = solved
    inverse = jnp.concatenate(panels, axis=0)
    mean_weights = jnp.sum(inverse * proj, axis=1, keepdims=True)
    rows = lax.broadcasted_iota(jnp.int32, (n, n), 0)
    weights = 0.5 * (n - 1.0) * inverse + jnp.where(rows == lanes, 0.5, 0.0) + mean_weights
    prior = ensemble_ref[...].astype(F32)
    prior_mean = jnp.mean(prior, axis=1, keepdims=True)
    moved = jnp.dot(prior - prior_mean, weights, precision=HIGH, preferred_element_type=F32)
    out_ref[...] = (prior_mean + moved).astype(BF16)


def per_device(ensemble, footprint, tile_index, tile_count, observed, obs_sigma):
    packed = summed_gram(ensemble, footprint, tile_index, tile_count, observed, obs_sigma)
    vmem = pl.BlockSpec(memory_space=pltpu.VMEM)
    return pl.pallas_call(
        posterior_kernel,
        out_shape=jax.ShapeDtypeStruct((256, 256), BF16),
        in_specs=[vmem, vmem],
        out_specs=vmem,
        scratch_shapes=[pltpu.VMEM((256, 256), F32)],
    )(packed.reshape(2, 128, 256), ensemble)


def solution(mesh):
    finer = Mesh(mesh.devices.reshape(4, 4, 16, 2), OBS_FLUX)
    placed = (
        P(OBS_FLUX, None),
        P(OBS, FLUX, None, None, None),
        P(OBS, FLUX, None),
        P(OBS, FLUX),
        P(OBS_FLUX),
        P(OBS_FLUX),
    )
    return jax.shard_map(
        per_device, mesh=finer, in_specs=placed, out_specs=P(OBS_FLUX, None), check_vma=False
    )
```
